128 devices in a mesh: row: 8 (over x, z_hi), col: 16 (over z_lo, y, core).
Axes of the slice: x: 4, y: 4, z: 4 (z_hi: 2, z_lo: 2; z = z_hi * 2 + z_lo), core: 2. Of those that a mesh axis runs over, the one named last changes fastest.
Arguments:
- vector: float32 [8192, 16384], P('row', 'col'), may hold values from -6 to 6
- links_alpha: int32 [64, 2], replicated, may hold values from 0 to 63, as said below
- alpha_values: float32 [64, 2, 128, 128], P('row'), may hold values from -0.375 to 0.375
- links_beta: int32 [128, 2], replicated, may hold values from 0 to 127, as said below
- beta_values: float32 [128, 2, 128, 128], P('col'), may hold values from -0.375 to 0.375
Outputs:
- sigma: float32 [8192, 16384], P('row', 'col')
The draws below stay inside these ranges and needn't reach their ends.
Inputs may be any that keep to these rules, and one draw needn't show every extreme that they name: Row g of links_alpha belongs to the index of row that owns alpha block g, which is g // 8; each entry names a block owned by index e // 8. Among the 16 entries in the rows of one index of row, at most 3 name blocks owned by any one index of row, and for each index some owner supplies exactly 3. Entries may repeat. Row h of links_beta belongs to the index of col that owns beta block h, which is h // 8; each entry names a block owned by index e // 8. Among the 16 entries in the rows of one index of col, at most 2 name blocks owned by any one index of col, and for each index some owner supplies exactly 2. Entries may repeat.
All inputs are finite; a program needn't handle non-finite values.
Results may differ from the reference program's by a relative error of at most 0.000053.
Values sent between devices are 32-bit elements; how exact they have to be, the bound alone decides.
No kernel may reach another device: no remote copies, remote signals or barrier semaphores. Data moves between devices by JAX's collectives and lax.ppermute only.
A program may use at most 128 MiB of HBM per device.

```python
import jax
import jax.numpy as jnp
from jax import lax

BLK = 128
A_DEV = 1024
B_DEV = 1024
NCONN_A = 2
NCONN_B = 2
NA = 8192
NB = 16384
NBA = 64
NBB = 128


def draw_links(key, total, per_device, connected):
    peers = total // per_device
    groups = per_device // BLK
    entries = groups * connected
    capacity = entries // peers + 1
    quarter = max(peers // 4, 1)
    position = jnp.arange(peers, dtype=jnp.int32)
    pattern = jnp.where(position < quarter, capacity, jnp.where(position < 2 * quarter, capacity - 2, capacity - 1))
    bounds = jnp.cumsum(pattern).astype(jnp.int32)
    slot_owner = jnp.searchsorted(bounds, jnp.arange(entries, dtype=jnp.int32), side='right').astype(jnp.int32)

    def one_device(device):
        subkey = jax.random.fold_in(key, device)
        owners = jax.random.permutation(jax.random.fold_in(subkey, 1), peers).astype(jnp.int32)
        source = owners[slot_owner]
        source = jax.random.permutation(jax.random.fold_in(subkey, 2), source)
        local_block = jax.random.randint(jax.random.fold_in(subkey, 3), (entries,), 0, groups, dtype=jnp.int32)
        return (source * groups + local_block).reshape(groups, connected)
    lists = jax.vmap(one_device)(jnp.arange(peers, dtype=jnp.int32))
    return lists.reshape(peers * groups, connected).astype(jnp.int32)


def draw_links_alpha(key, part):
    return draw_links(jax.random.fold_in(key, 11), NA, A_DEV, NCONN_A)


def draw_links_beta(key, part):
    return draw_links(jax.random.fold_in(key, 23), NB, B_DEV, NCONN_B)


def block_levels(rng, dims, shards, least, high):
    level, own = 1.0, jax.random.fold_in(rng, 6)
    for axis_at, blocks in shards:
        heights = jnp.exp(jax.random.uniform(jax.random.fold_in(own, axis_at), (blocks,), jnp.float32, least / len(shards), high / len(shards)))
        level = level * jnp.repeat(heights, dims[axis_at] // blocks).reshape([-1 if axis == axis_at else 1 for axis in range(len(dims))])
    return level


def gaussian(key, extent, width, bound, shards=(), kind=jnp.bfloat16):
    result = width * jax.random.normal(key, extent, jnp.float32)
    if shards:
        result = result * block_levels(key, extent, shards, -0.22, 0.18)
    return jnp.clip(result, -bound, bound).astype(kind)


def setup_inputs(seed: int = 0) -> dict:
    key_list = jax.random.split(jax.random.key(seed), 6)
    return {
        "vector": gaussian(key_list[0], (NA, NB), 1.0, 6.0, ((0, 8), (1, 16)), jnp.float32),
        "links_alpha": draw_links_alpha(jax.random.fold_in(key_list[5], 71), 0),
        "alpha_values": gaussian(key_list[2], (NBA, NCONN_A, BLK, BLK), (BLK * NCONN_A) ** -0.5, 0.375, ((0, 8),), jnp.float32),
        "links_beta": draw_links_beta(jax.random.fold_in(key_list[5], 71), 0),
        "beta_values": gaussian(key_list[4], (NBB, NCONN_B, BLK, BLK), (BLK * NCONN_B) ** -0.5, 0.375, ((0, 16),), jnp.float32),
    }


def reference(vector, links_alpha, alpha_values, links_beta, beta_values):
    row_blocks = vector.reshape(NBA, BLK, NB)

    def alpha_block(operands):
        indices, values = operands
        picked = jnp.take(row_blocks, indices, axis=0)
        return jnp.einsum("cij,cjk->ik", values, picked, precision=lax.Precision.HIGHEST)

    sigma_alpha = lax.map(alpha_block, (links_alpha, alpha_values)).reshape(NA, NB)
    col_blocks = vector.reshape(NA, NBB, BLK)

    def beta_block(operands):
        indices, values = operands
        picked = jnp.take(col_blocks, indices, axis=1)
        return jnp.einsum("ack,cik->ai", picked, values, precision=lax.Precision.HIGHEST)

    sigma_beta = lax.map(beta_block, (links_beta, beta_values))
    sigma_beta = jnp.transpose(sigma_beta, (1, 0, 2)).reshape(NA, NB)
    return sigma_alpha + sigma_beta
```

```python
import jax
import jax.numpy as jnp
from jax import lax
from jax.experimental import pallas as pl
from jax.experimental.pallas import tpu as pltpu
from jax.sharding import PartitionSpec as P


B = 128
AXES = ("row", "col")
HOPS = (1, 2, 3)
NX, NZH, NZL, NY, NK = 4, 2, 2, 4, 2


def _index(x, zh, zl, y, k):
    return (x * NZH + zh) * (NZL * NY * NK) + (zl * NY + y) * NK + k


def _pairs(move):
    pairs = []
    for x in range(NX):
        for zh in range(NZH):
            for zl in range(NZL):
                for y in range(NY):
                    for k in range(NK):
                        here = (x, zh, zl, y, k)
                        pairs.append((_index(*here), _index(*move(*here))))
    return pairs


def _z_next(x, zh, zl, y, k):
    z = (2 * zh + zl + (1 if zl == 1 else -1)) % 4
    return (x, z // 2, z % 2, y, k)


TO_CORE = _pairs(lambda x, zh, zl, y, k: (x, zh, zl, y, 1 - k))
TO_ZL = _pairs(lambda x, zh, zl, y, k: (x, zh, 1 - zl, y, k))
TO_ZNEXT = _pairs(_z_next)
TO_X = {d: _pairs(lambda x, zh, zl, y, k, d=d: ((x + d) % NX, zh, zl, y, k)) for d in HOPS}
TO_Y = {d: _pairs(lambda x, zh, zl, y, k, d=d: (x, zh, zl, (y + d) % NY, k)) for d in HOPS}


def _send(value, pairs):
    return lax.ppermute(value, AXES, pairs)


def _send_all(payloads, routes):
    return [_send(value, routes[d]) for d, value in zip(HOPS, payloads)]


def _ranks(mask):
    n = mask.shape[-1]
    earlier = jnp.arange(n)[:, None] < jnp.arange(n)[None, :]
    return jnp.sum(mask[..., :, None] * earlier.astype(jnp.int32), axis=-2)


def _lists(mask, pos, slots):
    n = mask.shape[-1]
    hit = mask[..., :, None] * (pos[..., :, None] == jnp.arange(slots)).astype(jnp.int32)
    return jnp.sum(hit * jnp.arange(n, dtype=jnp.int32)[:, None], axis=-2)


def _members(entries, blocks):
    hit = entries[:, :, None] == jnp.arange(blocks, dtype=jnp.int32)
    return jnp.max(hit.astype(jnp.int32), axis=1)


def alpha_tables(links, x, zh):
    wanted = links.reshape(NX * NZH, 16)
    mask = _members(wanted, 64).reshape(NX, NZH, NX, NZH, 8)
    mask = jnp.stack([mask[:, 0], mask[:, 1][:, :, ::-1]], axis=1)
    rank = _ranks(mask)
    mask = lax.dynamic_index_in_dim(mask, zh, 1, keepdims=False)
    rank = lax.dynamic_index_in_dim(rank, zh, 1, keepdims=False)
    sent_mask = lax.dynamic_index_in_dim(mask, x, 1, keepdims=False)
    sent_rank = lax.dynamic_index_in_dim(rank, x, 1, keepdims=False)
    lists = _lists(sent_mask, sent_rank, 3)
    lists = jnp.roll(lists, -x, axis=0)[1:]
    mine = lax.dynamic_index_in_dim(wanted, x * NZH + zh, 0, keepdims=False)
    source, block = mine // 8, mine % 8
    source_x, other = source // NZH, jnp.abs(source % NZH - zh)
    my_rank = lax.dynamic_index_in_dim(rank, x, 0, keepdims=False).reshape(-1)
    key = (source_x * 2 + other) * 8 + block
    slot = jnp.sum((key[:, None] == jnp.arange(my_rank.size)) * my_rank, axis=1)
    hop = (x - source_x) % NX
    place = jnp.where(hop == 0, other, 1 + hop + 3 * other)
    code = place * 32 + jnp.where(hop == 0, block, slot)
    return lists[:, 0].reshape(-1), lists[:, 1].reshape(-1), code.astype(jnp.int32)


def beta_tables(links, zl, y, k, first, second):
    wanted = links.reshape(NZL * NY, 32)
    mask = _members(wanted, 128).reshape(NZL, NY, NZL, NY, 16)
    mask = jnp.stack([mask[0], mask[1][:, ::-1]], axis=0)
    mask = jnp.swapaxes(mask, 2, 3)
    rank = _ranks(mask)
    own_count = jnp.sum(mask[:, :, :, 0], axis=-1)
    base = jnp.maximum(own_count, first)[..., None]
    pos = jnp.stack([rank[:, :, :, 0], base + rank[:, :, :, 1]], axis=3)
    mask = mask.reshape(NZL, NY, NY, 32)
    pos = pos.reshape(NZL, NY, NY, 32)
    far = (jnp.arange(NY)[:, None] != jnp.arange(NY)[None, :]).astype(jnp.int32)
    fits = jnp.max(mask * (pos + 1) * far[None, :, :, None]) <= first + second
    mask = lax.dynamic_index_in_dim(mask, zl, 0, keepdims=False)
    pos = lax.dynamic_index_in_dim(pos, zl, 0, keepdims=False)
    sent = _lists(
        lax.dynamic_index_in_dim(mask, y, 1, keepdims=False),
        lax.dynamic_index_in_dim(pos, y, 1, keepdims=False),
        first + second,
    )
    sent = jnp.roll(sent, -y, axis=0)[1:]
    core = (sent // 8) % 2
    sent = ((sent // 16) * 2 + jnp.abs(core - k)) * 32 + sent % 8
    mine = lax.dynamic_index_in_dim(wanted, zl * NY + y, 0, keepdims=False)
    chip, block = mine // 16, mine % 16
    source_y, other = chip % NY, jnp.abs(chip // NY - zl)
    my_pos = lax.dynamic_index_in_dim(pos, y, 0, keepdims=False).reshape(-1)
    key = (source_y * 2 + other) * 16 + block
    slot = jnp.sum((key[:, None] == jnp.arange(my_pos.size)) * my_pos, axis=1)
    hop = (y - source_y) % NY
    late = (slot >= first).astype(jnp.int32)
    near = (other * 2 + jnp.abs(block // 8 - k)) * 32 + block % 8
    code = jnp.where(hop == 0, near, (3 + hop + 3 * late) * 32 + slot - first * late)
    code = jnp.roll(code.reshape(2, 16), -k, axis=0).reshape(-1)
    return sent[:, :first].reshape(-1), sent[:, first:].reshape(-1), code.astype(jnp.int32), fits


def _rows(i):
    return pl.ds(pl.multiple_of(i * B, B), B)


def _core():
    return lax.rem(lax.axis_index("col"), NK).reshape(1)


def _fetch(code, options, dst, sem):
    place, at = code // 32, code % 32
    for number, source, half in options:
        test = place == number
        if half is not None:
            test = jnp.logical_and(test, at // 4 == half)

        @pl.when(test)
        def _(source=source):
            pltpu.make_async_copy(source(at), dst, sem).start()


def _wait(ref, sem):
    pltpu.make_async_copy(ref, ref, sem).wait()


ANY = pl.BlockSpec(memory_space=pl.ANY)
SMEM = pl.BlockSpec(memory_space=pltpu.SMEM)
VMEM = pl.BlockSpec(memory_space=pltpu.VMEM)


def _f32(*shape):
    return jax.ShapeDtypeStruct(shape, jnp.float32)


def _params():
    return pltpu.CompilerParams(vmem_limit_bytes=63 * 2**20)


def _cost(bytes_, flops=0):
    return pl.CostEstimate(flops=flops, bytes_accessed=bytes_, transcendentals=0)


def _gather(codes, slot_shape, slots, sources, options_of):
    count = 3 * slots

    def kernel(code_ref, k_ref, *refs):
        ins, outs = refs[: len(sources)], refs[len(sources) : len(sources) + 3]
        buf, in_sem, out_sem = refs[len(sources) + 3 :]
        options = options_of(ins, k_ref[0])
        for s in range(count):
            _fetch(code_ref[s], options, buf.at[s], in_sem.at[s])
        copies = []
        for s in range(count):
            _wait(buf.at[s], in_sem.at[s])
            copy = pltpu.make_async_copy(buf.at[s], outs[s // slots].at[s % slots], out_sem.at[s])
            copy.start()
            copies.append(copy)
        for copy in copies:
            copy.wait()

    size = 4 * count
    for n in slot_shape:
        size *= n
    return pl.pallas_call(
        kernel,
        out_shape=[_f32(slots, *slot_shape)] * 3,
        in_specs=[SMEM, SMEM] + [ANY] * len(sources),
        out_specs=[ANY] * 3,
        scratch_shapes=[
            pltpu.VMEM((count, *slot_shape), jnp.float32),
            pltpu.SemaphoreType.DMA((count,)),
            pltpu.SemaphoreType.DMA((count,)),
        ],
        compiler_params=_params(),
        cost_estimate=_cost(2 * size),
    )(codes, _core(), *sources)


def _pick(shapes, sources, picks_of):
    def kernel(k_ref, *refs):
        ins, outs = refs[: len(sources)], refs[len(sources) : len(sources) + len(shapes)]
        bufs = refs[len(sources) + len(shapes) : -2]
        in_sem, out_sem = refs[-2:]
        loads, stores = [], []
        for n, (source, number, at) in enumerate(picks_of(ins, k_ref[0])):
            buf, out = bufs[number], outs[number]
            if at is not None:
                buf, out = buf.at[at], out.at[at]
            loads.append(pltpu.make_async_copy(source, buf, in_sem.at[n]))
            stores.append(pltpu.make_async_copy(buf, out, out_sem.at[n]))
        for copy in loads:
            copy.start()
        for load, store in zip(loads, stores):
            load.wait()
            store.start()
        for copy in stores:
            copy.wait()

    size = 0
    for shape in shapes:
        words = 1
        for n in shape:
            words *= n
        size += 8 * words
    return pl.pallas_call(
        kernel,
        out_shape=[_f32(*shape) for shape in shapes],
        in_specs=[SMEM] + [ANY] * len(sources),
        out_specs=[ANY] * len(shapes),
        scratch_shapes=[pltpu.VMEM(shape, jnp.float32) for shape in shapes]
        + [pltpu.SemaphoreType.DMA((4,)), pltpu.SemaphoreType.DMA((4,))],
        compiler_params=_params(),
        cost_estimate=_cost(size),
    )(_core(), *sources)


def _split(v):
    high = v.astype(jnp.bfloat16)
    return high, (v - high.astype(jnp.float32)).astype(jnp.bfloat16)


def _dot3(a, b, dims):
    ah, al = _split(a)
    bh, bl = _split(b)

    def dot(p, q):
        return lax.dot_general(p, q, (dims, ((), ())), preferred_element_type=jnp.float32)

    return dot(ah, bh) + (dot(ah, bl) + dot(al, bh))


def _my_rows(r, k):
    return pl.ds(pl.multiple_of(r * 512 + k * 256, 256), 256)


def _half_rows(k):
    return pl.ds(pl.multiple_of(k * 256, 256), 256)


def _near(r, k, v, x0, q0, q1, x1):
    return [
        (0, lambda j: v.at[_my_rows(r, k), _rows(j)], None),
        (1, lambda j: x0.at[r, :, _rows(j)], None),
        (2, lambda j: q0.at[_half_rows(k), _rows(j % 4)], 0),
        (2, lambda j: q1.at[_half_rows(k), _rows(j % 4)], 1),
        (3, lambda j: x1.at[j // 4, :, _rows(j % 4)], None),
    ]


def beta_product(r, codes, mine, other, v, x0, q0, q1, x1, early, late):
    def kernel(code_ref, k_ref, mine_ref, other_ref, *refs):
        out_mine, out_other, buf, sem = refs[11:]
        options = _near(r, k_ref[0], *refs[0:5])
        options += [(4 + i, lambda s, i=i: refs[5 + i].at[s, r], None) for i in range(3)]
        options += [(7 + i, lambda s, i=i: refs[8 + i].at[s], None) for i in range(3)]
        for n in range(32):
            _fetch(code_ref[n], options, buf.at[n], sem.at[n])
        for h in range(16):
            w_ref, out = (mine_ref, out_mine) if h < 8 else (other_ref, out_other)
            w = jnp.concatenate([w_ref[h % 8, 0], w_ref[h % 8, 1]], axis=1)
            _wait(buf.at[2 * h], sem.at[2 * h])
            _wait(buf.at[2 * h + 1], sem.at[2 * h + 1])
            blocks = jnp.concatenate([buf[2 * h], buf[2 * h + 1]], axis=1)
            out[:, (h % 8) * B : (h % 8 + 1) * B] = _dot3(blocks, w, ((1,), (1,)))

    return pl.pallas_call(
        kernel,
        out_shape=[_f32(256, 1024)] * 2,
        in_specs=[SMEM, SMEM, VMEM, VMEM] + [ANY] * 11,
        out_specs=[VMEM, VMEM],
        scratch_shapes=[pltpu.VMEM((32, 256, B), jnp.float32), pltpu.SemaphoreType.DMA((32,))],
        compiler_params=_params(),
        cost_estimate=_cost(8 * 2**20, 3 * 32 * 2 * 256 * B * B),
    )(codes, _core(), mine, other, v, x0, q0, q1, x1, *early, *late)


def alpha_product(c, codes, values, v, q0, q1, own, late, tail=None):
    def kernel(code_ref, k_ref, w_ref, *refs):
        rest = refs[9:]
        out, buf, sem = rest[-3:]
        columns = pl.ds(c * 512, 512)
        v_ref, q0_ref, q1_ref = refs[0:3]
        options = [
            (0, lambda j: v_ref.at[_rows(j), columns], None),
            (1, lambda j: q0_ref.at[_rows(j % 4)], 0),
            (1, lambda j: q1_ref.at[_rows(j % 4)], 1),
        ]
        options += [(2 + i, lambda s, i=i: refs[3 + i].at[s, :, columns], None) for i in range(3)]
        options += [(5 + i, lambda s, i=i: refs[6 + i].at[s], None) for i in range(3)]
        for n in range(16):
            _fetch(code_ref[n], options, buf.at[n], sem.at[n])
        k = k_ref[0]
        for g in range(8):
            w = jnp.concatenate([w_ref[g, 0], w_ref[g, 1]], axis=1)
            _wait(buf.at[2 * g], sem.at[2 * g])
            _wait(buf.at[2 * g + 1], sem.at[2 * g + 1])
            product = _dot3(w, jnp.concatenate([buf[2 * g], buf[2 * g + 1]], axis=0), ((1,), (0,)))
            here = slice(g * B, (g + 1) * B)
            if tail is None:
                out[here] = product
                continue
            half, share, part = g // 4, (g % 4) // 2, slice((g % 2) * B, (g % 2 + 1) * B)

            def finish(beta_ref, product=product, here=here, part=part):
                for n in range(2):
                    there = slice(n * 512, (n + 1) * 512)
                    alpha = product if n == c else rest[0][here]
                    out[here, there] = alpha + beta_ref[part, there]

            @pl.when(k == share)
            def _(half=half, finish=finish):
                finish(rest[1 + half])

            @pl.when(k != share)
            def _(half=half, finish=finish):
                finish(rest[3 + half])

    extra = [] if tail is None else [tail[0], *tail[1], *tail[2]]
    return pl.pallas_call(
        kernel,
        out_shape=_f32(1024, 512 if tail is None else 1024),
        in_specs=[SMEM, SMEM, VMEM] + [ANY] * 9 + [VMEM] * len(extra),
        out_specs=VMEM,
        scratch_shapes=[pltpu.VMEM((16, B, 512), jnp.float32), pltpu.SemaphoreType.DMA((16,))],
        compiler_params=_params(),
        cost_estimate=_cost((7 if tail is None else 15) * 2**20, 3 * 16 * 2 * B * B * 512),
    )(codes, _core(), values, v, q0, q1, *own, *late, *extra)


def sigma_here(first, second, v, alpha_values, beta_values, alpha, beta):
    alpha_own, alpha_late, alpha_code = alpha
    beta_early, beta_late, beta_code = beta

    quadrants = [(0, 0), (1, 0), (0, 1), (1, 1)]
    (half,) = _pick(
        [(2, 256, 1024)],
        [v],
        lambda ins, k: [(ins[0].at[_my_rows(r, 1 - k)], 0, r) for r in range(2)],
    )
    x0 = _send(half, TO_CORE)
    pieces = _pick(
        [(512, 512)] * 4,
        [v],
        lambda ins, k: [
            (ins[0].at[r * 512 : (r + 1) * 512, c * 512 : (c + 1) * 512], n, None)
            for n, (r, c) in enumerate(quadrants)
        ],
    )
    zl = {(r, c): _send(piece, TO_ZL) for (r, c), piece in zip(quadrants, pieces)}
    other_values = _send(beta_values, TO_CORE)

    out = _gather(
        alpha_own, (B, 1024), 3, [v], lambda ins, k: [(0, lambda j: ins[0].at[_rows(j)], None)]
    )
    own = _send_all(out, TO_X)

    def early_options(ins, k):
        def of_v(j):
            return ins[0].at[:, _half_rows(k), _rows(j)]

        return [(0, of_v, None), (1, lambda j: ins[1].at[:, :, _rows(j)], None)]

    out = _gather(beta_early, (2, 256, B), first, [v.reshape(2, 512, 1024), x0], early_options)
    early = _send_all(out, TO_Y)

    zh = {(r, c): _send(zl[(r, c)], TO_ZNEXT) for r, c in quadrants}

    x1, late, x_late = {}, {}, {}
    for r in range(2):
        (half,) = _pick(
            [(2, 256, 512)],
            [zl[(r, 0)], zl[(r, 1)]],
            lambda ins, k: [(ins[c].at[_half_rows(1 - k)], 0, c) for c in range(2)],
        )
        x1[r] = _send(half, TO_CORE)
    for n in range(2):
        out = _gather(
            alpha_late,
            (B, 512),
            3,
            [zh[(0, n)], zh[(1, n)]],
            lambda ins, k: [(0, lambda j, i=i: ins[i].at[_rows(j % 4)], i) for i in range(2)],
        )
        x_late[n] = _send_all(out, TO_X)
        out = _gather(
            beta_late,
            (256, B),
            second,
            [v, x0, zl[(n, 0)], zl[(n, 1)], x1[n]],
            lambda ins, k, n=n: _near(n, k, *ins),
        )
        late[n] = _send_all(out, TO_Y)

    ours, theirs = [], []
    for r in range(2):
        a, b = beta_product(
            r, beta_code, beta_values, other_values, v, x0, zl[(r, 0)], zl[(r, 1)], x1[r], early, late[r]
        )
        ours.append(a)
        theirs.append(_send(b, TO_CORE))
    part = alpha_product(0, alpha_code, alpha_values, v, zh[(0, 0)], zh[(1, 0)], own, x_late[0])
    return alpha_product(
        1, alpha_code, alpha_values, v, zh[(0, 1)], zh[(1, 1)], own, x_late[1], (part, ours, theirs)
    )


def per_device(vector, links_alpha, alpha_values, links_beta, beta_values):
    row, col = lax.axis_index("row"), lax.axis_index("col")
    x, zh = row // NZH, row % NZH
    zl, y, k = col // (NY * NK), (col // NK) % NY, col % NK
    alpha = alpha_tables(links_alpha, x, zh)
    *beta, _ = beta_tables(links_beta, zl, y, k, 8, 8)
    return sigma_here(8, 8, vector, alpha_values, beta_values, alpha, beta)


def solution(mesh):
    placed = (P("row", "col"), P(), P("row", None, None, None), P(), P("col", None, None, None))
    return jax.shard_map(per_device, mesh=mesh, in_specs=placed, out_specs=P("row", "col"), check_vma=False)
```

```python
import jax
import jax.numpy as jnp
from jax import lax
from jax.experimental import pallas as pl
from jax.experimental.pallas import tpu as pltpu
from jax.sharding import PartitionSpec as P


B = 128
AXES = ("row", "col")
HOPS = (1, 2, 3)
EARLY, LATE = 5, 7
NX, NZH, NZL, NY, NK = 4, 2, 2, 4, 2


def _index(x, zh, zl, y, k):
    return (x * NZH + zh) * (NZL * NY * NK) + (zl * NY + y) * NK + k


def _pairs(move):
    pairs = []
    for x in range(NX):
        for zh in range(NZH):
            for zl in range(NZL):
                for y in range(NY):
                    for k in range(NK):
                        here = (x, zh, zl, y, k)
                        pairs.append((_index(*here), _index(*move(*here))))
    return pairs


def _z_next(x, zh, zl, y, k):
    z = (2 * zh + zl + (1 if zl == 1 else -1)) % 4
    return (x, z // 2, z % 2, y, k)


TO_CORE = _pairs(lambda x, zh, zl, y, k: (x, zh, zl, y, 1 - k))
TO_ZL = _pairs(lambda x, zh, zl, y, k: (x, zh, 1 - zl, y, k))
TO_ZNEXT = _pairs(_z_next)
TO_X = {d: _pairs(lambda x, zh, zl, y, k, d=d: ((x + d) % NX, zh, zl, y, k)) for d in HOPS}
TO_Y = {d: _pairs(lambda x, zh, zl, y, k, d=d: (x, zh, zl, (y + d) % NY, k)) for d in HOPS}


def _send(value, pairs):
    return lax.ppermute(value, AXES, pairs)


def _send_all(payloads, routes):
    return [_send(value, routes[d]) for d, value in zip(HOPS, payloads)]


def _ranks(mask):
    n = mask.shape[-1]
    earlier = jnp.arange(n)[:, None] < jnp.arange(n)[None, :]
    return jnp.sum(mask[..., :, None] * earlier.astype(jnp.int32), axis=-2)


def _lists(mask, pos, slots):
    n = mask.shape[-1]
    hit = mask[..., :, None] * (pos[..., :, None] == jnp.arange(slots)).astype(jnp.int32)
    return jnp.sum(hit * jnp.arange(n, dtype=jnp.int32)[:, None], axis=-2)


def _members(entries, blocks):
    hit = entries[:, :, None] == jnp.arange(blocks, dtype=jnp.int32)
    return jnp.max(hit.astype(jnp.int32), axis=1)


def alpha_tables(links, x, zh):
    wanted = links.reshape(NX * NZH, 16)
    mask = _members(wanted, 64).reshape(NX, NZH, NX, NZH, 8)
    mask = jnp.stack([mask[:, 0], mask[:, 1][:, :, ::-1]], axis=1)
    rank = _ranks(mask)
    mask = lax.dynamic_index_in_dim(mask, zh, 1, keepdims=False)
    rank = lax.dynamic_index_in_dim(rank, zh, 1, keepdims=False)
    sent_mask = lax.dynamic_index_in_dim(mask, x, 1, keepdims=False)
    sent_rank = lax.dynamic_index_in_dim(rank, x, 1, keepdims=False)
    lists = _lists(sent_mask, sent_rank, 3)
    lists = jnp.roll(lists, -x, axis=0)[1:]
    mine = lax.dynamic_index_in_dim(wanted, x * NZH + zh, 0, keepdims=False)
    source, block = mine // 8, mine % 8
    source_x, other = source // NZH, jnp.abs(source % NZH - zh)
    my_rank = lax.dynamic_index_in_dim(rank, x, 0, keepdims=False).reshape(-1)
    key = (source_x * 2 + other) * 8 + block
    slot = jnp.sum((key[:, None] == jnp.arange(my_rank.size)) * my_rank, axis=1)
    hop = (x - source_x) % NX
    place = jnp.where(hop == 0, other, 1 + hop + 3 * other)
    code = place * 32 + jnp.where(hop == 0, block, slot)
    return lists[:, 0].reshape(-1), lists[:, 1].reshape(-1), code.astype(jnp.int32)


def beta_tables(links, zl, y, k):
    wanted = links.reshape(NZL * NY, 32)
    mask = _members(wanted, 128).reshape(NZL, NY, NZL, NY, 16)
    mask = jnp.stack([mask[0], mask[1][:, ::-1]], axis=0)
    mask = jnp.swapaxes(mask, 2, 3)
    rank = _ranks(mask)
    own_count = jnp.sum(mask[:, :, :, 0], axis=-1)
    base = jnp.maximum(own_count, EARLY)[..., None]
    pos = jnp.stack([rank[:, :, :, 0], base + rank[:, :, :, 1]], axis=3)
    mask = mask.reshape(NZL, NY, NY, 32)
    pos = pos.reshape(NZL, NY, NY, 32)
    far = (jnp.arange(NY)[:, None] != jnp.arange(NY)[None, :]).astype(jnp.int32)
    fits = jnp.max(mask * (pos + 1) * far[None, :, :, None]) <= EARLY + LATE
    mask = lax.dynamic_index_in_dim(mask, zl, 0, keepdims=False)
    pos = lax.dynamic_index_in_dim(pos, zl, 0, keepdims=False)
    sent = _lists(
        lax.dynamic_index_in_dim(mask, y, 1, keepdims=False),
        lax.dynamic_index_in_dim(pos, y, 1, keepdims=False),
        16,
    )
    sent = jnp.roll(sent, -y, axis=0)[1:]
    core = (sent // 8) % 2
    sent = ((sent // 16) * 2 + jnp.abs(core - k)) * 32 + sent % 8
    mine = lax.dynamic_index_in_dim(wanted, zl * NY + y, 0, keepdims=False)
    chip, block = mine // 16, mine % 16
    source_y, other = chip % NY, jnp.abs(chip // NY - zl)
    my_pos = lax.dynamic_index_in_dim(pos, y, 0, keepdims=False).reshape(-1)
    key = (source_y * 2 + other) * 16 + block
    slot = jnp.sum((key[:, None] == jnp.arange(my_pos.size)) * my_pos, axis=1)
    hop = (y - source_y) % NY
    late, extra = (slot >= EARLY).astype(jnp.int32), (slot >= EARLY + LATE).astype(jnp.int32)
    near = (other * 2 + jnp.abs(block // 8 - k)) * 32 + block % 8
    code = jnp.where(hop == 0, near, (3 + hop + 3 * late + 3 * extra) * 32 + slot - EARLY * late - LATE * extra)
    code = jnp.roll(code.reshape(2, 16), -k, axis=0).reshape(-1)
    lists = [part.reshape(-1) for part in jnp.split(sent, [EARLY, EARLY + LATE], axis=1)]
    return (*lists, code.astype(jnp.int32), fits)


def _rows(i):
    return pl.ds(pl.multiple_of(i * B, B), B)


def _core():
    return lax.rem(lax.axis_index("col"), NK).reshape(1)


def _fetch(code, options, dst, sem):
    place, at = code // 32, code % 32
    for number, source, half in options:
        test = place == number
        if half is not None:
            test = jnp.logical_and(test, at // 4 == half)

        @pl.when(test)
        def _(source=source):
            pltpu.make_async_copy(source(at), dst, sem).start()


def _wait(ref, sem):
    pltpu.make_async_copy(ref, ref, sem).wait()


ANY = pl.BlockSpec(memory_space=pl.ANY)
SMEM = pl.BlockSpec(memory_space=pltpu.SMEM)
VMEM = pl.BlockSpec(memory_space=pltpu.VMEM)


def _f32(*shape):
    return jax.ShapeDtypeStruct(shape, jnp.float32)


def _params():
    return pltpu.CompilerParams(vmem_limit_bytes=63 * 2**20)


def _cost(bytes_, flops=0):
    return pl.CostEstimate(flops=flops, bytes_accessed=bytes_, transcendentals=0)


def _gather(codes, slot_shape, slots, sources, options_of):
    count = 3 * slots

    def kernel(code_ref, k_ref, *refs):
        ins, outs = refs[: len(sources)], refs[len(sources) : len(sources) + 3]
        buf, in_sem, out_sem = refs[len(sources) + 3 :]
        options = options_of(ins, k_ref[0])

        def load(s, _):
            _fetch(code_ref[s], options, buf.at[s], in_sem.at[s])

        lax.fori_loop(0, count, load, None)
        for hop, out in enumerate(outs):

            def store(s, _, hop=hop, out=out):
                n = hop * slots + s
                _wait(buf.at[n], in_sem.at[n])
                pltpu.make_async_copy(buf.at[n], out.at[s], out_sem.at[n]).start()

            lax.fori_loop(0, slots, store, None)

        def finish(s, _):
            _wait(buf.at[s], out_sem.at[s])

        lax.fori_loop(0, count, finish, None)

    size = 4 * count
    for n in slot_shape:
        size *= n
    return pl.pallas_call(
        kernel,
        out_shape=[_f32(slots, *slot_shape)] * 3,
        in_specs=[SMEM, SMEM] + [ANY] * len(sources),
        out_specs=[ANY] * 3,
        scratch_shapes=[
            pltpu.VMEM((count, *slot_shape), jnp.float32),
            pltpu.SemaphoreType.DMA((count,)),
            pltpu.SemaphoreType.DMA((count,)),
        ],
        compiler_params=_params(),
        cost_estimate=_cost(2 * size),
    )(codes, _core(), *sources)


def _pick(shapes, sources, picks_of):
    def kernel(k_ref, *refs):
        ins, outs = refs[: len(sources)], refs[len(sources) : len(sources) + len(shapes)]
        bufs = refs[len(sources) + len(shapes) : -2]
        in_sem, out_sem = refs[-2:]
        loads, stores = [], []
        for n, (source, number, at) in enumerate(picks_of(ins, k_ref[0])):
            buf, out = bufs[number], outs[number]
            if at is not None:
                buf, out = buf.at[at], out.at[at]
            loads.append(pltpu.make_async_copy(source, buf, in_sem.at[n]))
            stores.append(pltpu.make_async_copy(buf, out, out_sem.at[n]))
        for copy in loads:
            copy.start()
        for load, store in zip(loads, stores):
            load.wait()
            store.start()
        for copy in stores:
            copy.wait()

    size = 0
    for shape in shapes:
        words = 1
        for n in shape:
            words *= n
        size += 8 * words
    return pl.pallas_call(
        kernel,
        out_shape=[_f32(*shape) for shape in shapes],
        in_specs=[SMEM] + [ANY] * len(sources),
        out_specs=[ANY] * len(shapes),
        scratch_shapes=[pltpu.VMEM(shape, jnp.float32) for shape in shapes]
        + [pltpu.SemaphoreType.DMA((4,)), pltpu.SemaphoreType.DMA((4,))],
        compiler_params=_params(),
        cost_estimate=_cost(size),
    )(_core(), *sources)


def _split(v):
    high = v.astype(jnp.bfloat16)
    return high, (v - high.astype(jnp.float32)).astype(jnp.bfloat16)


def _dot3(a, b, dims):
    ah, al = _split(a)
    bh, bl = _split(b)

    def dot(p, q):
        return lax.dot_general(p, q, (dims, ((), ())), preferred_element_type=jnp.float32)

    return dot(ah, bh) + (dot(ah, bl) + dot(al, bh))


def _my_rows(r, k):
    return pl.ds(pl.multiple_of(r * 512 + k * 256, 256), 256)


def _half_rows(k):
    return pl.ds(pl.multiple_of(k * 256, 256), 256)


def _near(r, k, v, x0, q0, q1, x1):
    return [
        (0, lambda j: v.at[_my_rows(r, k), _rows(j)], None),
        (1, lambda j: x0.at[r, :, _rows(j)], None),
        (2, lambda j: q0.at[_half_rows(k), _rows(j % 4)], 0),
        (2, lambda j: q1.at[_half_rows(k), _rows(j % 4)], 1),
        (3, lambda j: x1.at[j // 4, :, _rows(j % 4)], None),
    ]


def beta_product(r, codes, mine, other, v, x0, q0, q1, x1, early, late, extra):
    def kernel(code_ref, k_ref, mine_ref, other_ref, *refs):
        out_mine, out_other, buf, sem = refs[14:]
        options = _near(r, k_ref[0], *refs[0:5])
        options += [(4 + i, lambda s, i=i: refs[5 + i].at[s, r], None) for i in range(3)]
        options += [(7 + i, lambda s, i=i: refs[8 + i].at[s], None) for i in range(3)]
        options += [(10 + i, lambda s, i=i: refs[11 + i].at[s, r], None) for i in range(3)]

        def load(n, _):
            _fetch(code_ref[n], options, buf.at[n], sem.at[n])

        lax.fori_loop(0, 32, load, None)
        for first, w_ref, out in ((0, mine_ref, out_mine), (16, other_ref, out_other)):

            def block(h, _, first=first, w_ref=w_ref, out=out):
                n = first + 2 * h
                w = jnp.concatenate([w_ref[h, 0], w_ref[h, 1]], axis=1)
                _wait(buf.at[n], sem.at[n])
                _wait(buf.at[n + 1], sem.at[n + 1])
                blocks = jnp.concatenate([buf[n], buf[n + 1]], axis=1)
                out[:, _rows(h)] = _dot3(blocks, w, ((1,), (1,)))

            lax.fori_loop(0, 8, block, None, unroll=2)

    return pl.pallas_call(
        kernel,
        out_shape=[_f32(256, 1024)] * 2,
        in_specs=[SMEM, SMEM, VMEM, VMEM] + [ANY] * 14,
        out_specs=[VMEM, VMEM],
        scratch_shapes=[pltpu.VMEM((32, 256, B), jnp.float32), pltpu.SemaphoreType.DMA((32,))],
        compiler_params=_params(),
        cost_estimate=_cost(8 * 2**20, 3 * 32 * 2 * 256 * B * B),
    )(codes, _core(), mine, other, v, x0, q0, q1, x1, *early, *late, *extra)


def alpha_product(c, codes, values, v, q0, q1, own, late, tail=None):
    def kernel(code_ref, k_ref, w_ref, *refs):
        rest = refs[9:]
        out, buf, sem = rest[-3:]
        columns = pl.ds(c * 512, 512)
        v_ref, q0_ref, q1_ref = refs[0:3]
        options = [
            (0, lambda j: v_ref.at[_rows(j), columns], None),
            (1, lambda j: q0_ref.at[_rows(j % 4)], 0),
            (1, lambda j: q1_ref.at[_rows(j % 4)], 1),
        ]
        options += [(2 + i, lambda s, i=i: refs[3 + i].at[s, :, columns], None) for i in range(3)]
        options += [(5 + i, lambda s, i=i: refs[6 + i].at[s], None) for i in range(3)]

        def load(n, _):
            _fetch(code_ref[n], options, buf.at[n], sem.at[n])

        lax.fori_loop(0, 16, load, None)
        k = k_ref[0]
        for g in range(8):
            w = jnp.concatenate([w_ref[g, 0], w_ref[g, 1]], axis=1)
            _wait(buf.at[2 * g], sem.at[2 * g])
            _wait(buf.at[2 * g + 1], sem.at[2 * g + 1])
            product = _dot3(w, jnp.concatenate([buf[2 * g], buf[2 * g + 1]], axis=0), ((1,), (0,)))
            here = slice(g * B, (g + 1) * B)
            if tail is None:
                out[here] = product
                continue
            half, share, part = g // 4, (g % 4) // 2, slice((g % 2) * B, (g % 2 + 1) * B)

            def finish(beta_ref, product=product, here=here, part=part):
                for n in range(2):
                    there = slice(n * 512, (n + 1) * 512)
                    alpha = product if n == c else rest[0][here]
                    out[here, there] = alpha + beta_ref[part, there]

            @pl.when(k == share)
            def _(half=half, finish=finish):
                finish(rest[1 + half])

            @pl.when(k != share)
            def _(half=half, finish=finish):
                finish(rest[3 + half])

    extra = [] if tail is None else [tail[0], *tail[1], *tail[2]]
    return pl.pallas_call(
        kernel,
        out_shape=_f32(1024, 512 if tail is None else 1024),
        in_specs=[SMEM, SMEM, VMEM] + [ANY] * 9 + [VMEM] * len(extra),
        out_specs=VMEM,
        scratch_shapes=[pltpu.VMEM((16, B, 512), jnp.float32), pltpu.SemaphoreType.DMA((16,))],
        compiler_params=_params(),
        cost_estimate=_cost((7 if tail is None else 15) * 2**20, 3 * 16 * 2 * B * B * 512),
    )(codes, _core(), values, v, q0, q1, *own, *late, *extra)


def sigma_here(v, alpha_values, beta_values, alpha, beta):
    alpha_own, alpha_late, alpha_code = alpha
    beta_early, beta_late, beta_extra, beta_code, fits = beta

    quadrants = [(0, 0), (0, 1), (1, 0), (1, 1)]
    (half,) = _pick([(2, 256, 1024)], [v], lambda ins, k: [(ins[0].at[_my_rows(r, 1 - k)], 0, r) for r in range(2)])
    x0 = _send(half, TO_CORE)
    pieces = _pick(
        [(512, 512)] * 4,
        [v],
        lambda ins, k: [
            (ins[0].at[r * 512 : (r + 1) * 512, c * 512 : (c + 1) * 512], n, None)
            for n, (r, c) in enumerate(quadrants)
        ],
    )
    zl = {(r, c): _send(piece, TO_ZL) for (r, c), piece in zip(quadrants, pieces)}
    other_values = _send(beta_values, TO_CORE)

    out = _gather(alpha_own, (B, 1024), 3, [v], lambda ins, k: [(0, lambda j: ins[0].at[_rows(j)], None)])
    own = _send_all(out, TO_X)

    def early_options(ins, k):
        def of_v(j):
            return ins[0].at[:, _half_rows(k), _rows(j)]

        return [(0, of_v, None), (1, lambda j: ins[1].at[:, :, _rows(j)], None)]

    out = _gather(beta_early, (2, 256, B), EARLY, [v.reshape(2, 512, 1024), x0], early_options)
    early = _send_all(out, TO_Y)

    zh = {(r, c): _send(zl[(r, c)], TO_ZNEXT) for r, c in quadrants}

    x1, late, x_late = {}, {}, {}
    for r in range(2):
        (half,) = _pick(
            [(2, 256, 512)],
            [zl[(r, 0)], zl[(r, 1)]],
            lambda ins, k: [(ins[c].at[_half_rows(1 - k)], 0, c) for c in range(2)],
        )
        x1[r] = _send(half, TO_CORE)
    for n in range(2):
        out = _gather(
            alpha_late,
            (B, 512),
            3,
            [zh[(0, n)], zh[(1, n)]],
            lambda ins, k: [(0, lambda j, i=i: ins[i].at[_rows(j % 4)], i) for i in range(2)],
        )
        x_late[n] = _send_all(out, TO_X)
        out = _gather(
            beta_late, (256, B), LATE, [v, x0, zl[(n, 0)], zl[(n, 1)], x1[n]], lambda ins, k, n=n: _near(n, k, *ins)
        )
        late[n] = _send_all(out, TO_Y)

    def send_extra():
        halves = []
        for r in range(2):
            halves.append(
                _gather(
                    beta_extra,
                    (256, B),
                    16 - EARLY - LATE,
                    [v, x0, zl[(r, 0)], zl[(r, 1)], x1[r]],
                    lambda ins, k, r=r: _near(r, k, *ins),
                )
            )
        return tuple(_send_all([jnp.stack(pair, axis=1) for pair in zip(*halves)], TO_Y))

    def skip_extra():
        return tuple(jnp.zeros((16 - EARLY - LATE, 2, 256, B), jnp.float32) for _ in HOPS)

    extra = lax.cond(fits, skip_extra, send_extra)

    ours, theirs = [], []
    for r in range(2):
        a, b = beta_product(
            r, beta_code, beta_values, other_values, v, x0, zl[(r, 0)], zl[(r, 1)], x1[r], early, late[r], extra
        )
        ours.append(a)
        theirs.append(_send(b, TO_CORE))
    part = alpha_product(0, alpha_code, alpha_values, v, zh[(0, 0)], zh[(1, 0)], own, x_late[0])
    return alpha_product(
        1, alpha_code, alpha_values, v, zh[(0, 1)], zh[(1, 1)], own, x_late[1], (part, ours, theirs)
    )


def per_device(vector, links_alpha, alpha_values, links_beta, beta_values):
    row, col = lax.axis_index("row"), lax.axis_index("col")
    x, zh = row // NZH, row % NZH
    zl, y, k = col // (NY * NK), (col // NK) % NY, col % NK
    alpha = alpha_tables(links_alpha, x, zh)
    beta = beta_tables(links_beta, zl, y, k)
    return sigma_here(vector, alpha_values, beta_values, alpha, beta)


def solution(mesh):
    placed = (P("row", "col"), P(), P("row", None, None, None), P(), P("col", None, None, None))
    return jax.shard_map(per_device, mesh=mesh, in_specs=placed, out_specs=P("row", "col"), check_vma=False)
```

```python
import jax
import jax.numpy as jnp
from jax import lax
from jax.experimental import pallas as pl
from jax.experimental.pallas import tpu as pltpu
from jax.sharding import PartitionSpec as P


B = 128
AXES = ("row", "col")
HOPS = (1, 2, 3)
STARTS, SLOTS = (0, 5, 11, 12), (5, 6, 1, 4)
EARLY, LATE, *EXTRA = SLOTS
ALPHA_OWN, ALPHA_LATE, ALPHA_CODE, BETA_LISTS = 1, 10, 19, 35
BETA_CODE = BETA_LISTS + 3 * 16
NX, NZH, NZL, NY, NK = 4, 2, 2, 4, 2


def _index(x, zh, zl, y, k):
    return (x * NZH + zh) * (NZL * NY * NK) + (zl * NY + y) * NK + k


def _pairs(move):
    pairs = []
    for x in range(NX):
        for zh in range(NZH):
            for zl in range(NZL):
                for y in range(NY):
                    for k in range(NK):
                        here = (x, zh, zl, y, k)
                        pairs.append((_index(*here), _index(*move(*here))))
    return pairs


def _z_next(x, zh, zl, y, k):
    z = (2 * zh + zl + (1 if zl == 1 else -1)) % 4
    return (x, z // 2, z % 2, y, k)


TO_CORE = _pairs(lambda x, zh, zl, y, k: (x, zh, zl, y, 1 - k))
TO_ZL = _pairs(lambda x, zh, zl, y, k: (x, zh, 1 - zl, y, k))
TO_ZNEXT = _pairs(_z_next)
TO_X = {d: _pairs(lambda x, zh, zl, y, k, d=d: ((x + d) % NX, zh, zl, y, k)) for d in HOPS}
TO_Y = {d: _pairs(lambda x, zh, zl, y, k, d=d: (x, zh, zl, (y + d) % NY, k)) for d in HOPS}


def _send(value, pairs):
    return lax.ppermute(value, AXES, pairs)


def _send_all(payloads, routes):
    return [_send(value, routes[d]) for d, value in zip(HOPS, payloads)]


def _ranks(mask):
    n = mask.shape[-1]
    earlier = jnp.arange(n)[:, None] < jnp.arange(n)[None, :]
    return jnp.sum(mask[..., :, None] * earlier.astype(jnp.int32), axis=-2)


def _lists(mask, pos, slots):
    n = mask.shape[-1]
    hit = mask[..., :, None] * (pos[..., :, None] == jnp.arange(slots)).astype(jnp.int32)
    return jnp.sum(hit * jnp.arange(n, dtype=jnp.int32)[:, None], axis=-2)


def _members(entries, blocks):
    hit = entries[:, :, None] == jnp.arange(blocks, dtype=jnp.int32)
    return jnp.max(hit.astype(jnp.int32), axis=1)


def alpha_tables(links, x, zh):
    wanted = links.reshape(NX * NZH, 16)
    mask = _members(wanted, 64).reshape(NX, NZH, NX, NZH, 8)
    mask = jnp.stack([mask[:, 0], mask[:, 1][:, :, ::-1]], axis=1)
    rank = _ranks(mask)
    mask = lax.dynamic_index_in_dim(mask, zh, 1, keepdims=False)
    rank = lax.dynamic_index_in_dim(rank, zh, 1, keepdims=False)
    sent_mask = lax.dynamic_index_in_dim(mask, x, 1, keepdims=False)
    sent_rank = lax.dynamic_index_in_dim(rank, x, 1, keepdims=False)
    lists = _lists(sent_mask, sent_rank, 3)
    lists = jnp.roll(lists, -x, axis=0)[1:]
    mine = lax.dynamic_index_in_dim(wanted, x * NZH + zh, 0, keepdims=False)
    source, block = mine // 8, mine % 8
    source_x, other = source // NZH, jnp.abs(source % NZH - zh)
    my_rank = lax.dynamic_index_in_dim(rank, x, 0, keepdims=False).reshape(-1)
    key = (source_x * 2 + other) * 8 + block
    slot = jnp.sum((key[:, None] == jnp.arange(my_rank.size)) * my_rank, axis=1)
    hop = (x - source_x) % NX
    place = jnp.where(hop == 0, other, 1 + hop + 3 * other)
    code = place * 32 + jnp.where(hop == 0, block, slot)
    return lists[:, 0].reshape(-1), lists[:, 1].reshape(-1), code.astype(jnp.int32)


def beta_tables(links, zl, y, k):
    wanted = links.reshape(NZL * NY, 32)
    mask = _members(wanted, 128).reshape(NZL, NY, NZL, NY, 16)
    mask = jnp.stack([mask[0], mask[1][:, ::-1]], axis=0)
    mask = jnp.swapaxes(mask, 2, 3)
    rank = _ranks(mask)
    own_count = jnp.sum(mask[:, :, :, 0], axis=-1)
    base = jnp.maximum(own_count, EARLY)[..., None]
    pos = jnp.stack([rank[:, :, :, 0], base + rank[:, :, :, 1]], axis=3)
    mask = mask.reshape(NZL, NY, NY, 32)
    pos = pos.reshape(NZL, NY, NY, 32)
    far = (jnp.arange(NY)[:, None] != jnp.arange(NY)[None, :]).astype(jnp.int32)
    need = jnp.max(mask * (pos + 1) * far[None, :, :, None])
    mask = lax.dynamic_index_in_dim(mask, zl, 0, keepdims=False)
    pos = lax.dynamic_index_in_dim(pos, zl, 0, keepdims=False)
    sent = _lists(
        lax.dynamic_index_in_dim(mask, y, 1, keepdims=False),
        lax.dynamic_index_in_dim(pos, y, 1, keepdims=False),
        16,
    )
    sent = jnp.roll(sent, -y, axis=0)[1:]
    core = (sent // 8) % 2
    sent = ((sent // 16) * 2 + jnp.abs(core - k)) * 32 + sent % 8
    mine = lax.dynamic_index_in_dim(wanted, zl * NY + y, 0, keepdims=False)
    chip, block = mine // 16, mine % 16
    source_y, other = chip % NY, jnp.abs(chip // NY - zl)
    my_pos = lax.dynamic_index_in_dim(pos, y, 0, keepdims=False).reshape(-1)
    key = (source_y * 2 + other) * 16 + block
    slot = jnp.sum((key[:, None] == jnp.arange(my_pos.size)) * my_pos, axis=1)
    hop = (y - source_y) % NY
    passed = [(slot >= start).astype(jnp.int32) for start in STARTS[1:]]
    level = sum(passed)
    at = slot - sum((start - before) * p for before, start, p in zip(STARTS, STARTS[1:], passed))
    near = (other * 2 + jnp.abs(block // 8 - k)) * 32 + block % 8
    code = jnp.where(hop == 0, near, (3 + hop + 3 * level) * 32 + at)
    code = jnp.roll(code.reshape(2, 16), -k, axis=0).reshape(-1)
    lists = [part.reshape(-1) for part in jnp.split(sent, STARTS[1:], axis=1)]
    return (*lists, code.astype(jnp.int32), need)


def _rows(i):
    return pl.ds(pl.multiple_of(i * B, B), B)


def _fetch(code, options, dst, sem):
    place, at = code // 32, code % 32
    for group in options:
        first, last = group[0][0], group[-1][0]

        @pl.when(jnp.logical_and(place >= first, place <= last))
        def _(group=group):
            for number, source, half in group:
                test = place == number
                if half is not None:
                    test = jnp.logical_and(test, at // 4 == half)

                @pl.when(test)
                def _(source=source):
                    pltpu.make_async_copy(source(at), dst, sem).start()


def _wait(ref, sem):
    pltpu.make_async_copy(ref, ref, sem).wait()


ANY = pl.BlockSpec(memory_space=pl.ANY)
SMEM = pl.BlockSpec(memory_space=pltpu.SMEM)
VMEM = pl.BlockSpec(memory_space=pltpu.VMEM)


def _f32(*shape):
    return jax.ShapeDtypeStruct(shape, jnp.float32)


def _params():
    return pltpu.CompilerParams(vmem_limit_bytes=63 * 2**20)


def _cost(bytes_, flops=0):
    return pl.CostEstimate(flops=flops, bytes_accessed=bytes_, transcendentals=0)


def _gather(table, start, slot_shape, slots, sources, options_of):
    count = 3 * slots

    def kernel(table_ref, *refs):
        ins, outs = refs[: len(sources)], refs[len(sources) : len(sources) + 3]
        buf, in_sem, out_sem = refs[len(sources) + 3 :]
        options = options_of(ins, table_ref[0])

        def load(s, _):
            _fetch(table_ref[start + s], options, buf.at[s], in_sem.at[s])

        lax.fori_loop(0, count, load, None)
        for hop, out in enumerate(outs):

            def store(s, _, hop=hop, out=out):
                n = hop * slots + s
                _wait(buf.at[n], in_sem.at[n])
                pltpu.make_async_copy(buf.at[n], out.at[s], out_sem.at[n]).start()

            lax.fori_loop(0, slots, store, None)

        def finish(s, _):
            _wait(buf.at[s], out_sem.at[s])

        lax.fori_loop(0, count, finish, None)

    size = 4 * count
    for n in slot_shape:
        size *= n
    return pl.pallas_call(
        kernel,
        out_shape=[_f32(slots, *slot_shape)] * 3,
        in_specs=[SMEM] + [ANY] * len(sources),
        out_specs=[ANY] * 3,
        scratch_shapes=[
            pltpu.VMEM((count, *slot_shape), jnp.float32),
            pltpu.SemaphoreType.DMA((count,)),
            pltpu.SemaphoreType.DMA((count,)),
        ],
        compiler_params=_params(),
        cost_estimate=_cost(2 * size),
    )(table, *sources)


def _pick(core, shapes, sources, picks_of):
    def kernel(k_ref, *refs):
        ins, outs = refs[: len(sources)], refs[len(sources) : len(sources) + len(shapes)]
        bufs = refs[len(sources) + len(shapes) : -2]
        in_sem, out_sem = refs[-2:]
        loads, stores = [], []
        for n, (source, number, at) in enumerate(picks_of(ins, k_ref[0])):
            buf, out = bufs[number], outs[number]
            if at is not None:
                buf, out = buf.at[at], out.at[at]
            loads.append(pltpu.make_async_copy(source, buf, in_sem.at[n]))
            stores.append(pltpu.make_async_copy(buf, out, out_sem.at[n]))
        for copy in loads:
            copy.start()
        for load, store in zip(loads, stores):
            load.wait()
            store.start()
        for copy in stores:
            copy.wait()

    size = 0
    for shape in shapes:
        words = 1
        for n in shape:
            words *= n
        size += 8 * words
    return pl.pallas_call(
        kernel,
        out_shape=[_f32(*shape) for shape in shapes],
        in_specs=[SMEM] + [ANY] * len(sources),
        out_specs=[ANY] * len(shapes),
        scratch_shapes=[pltpu.VMEM(shape, jnp.float32) for shape in shapes]
        + [pltpu.SemaphoreType.DMA((4,)), pltpu.SemaphoreType.DMA((4,))],
        compiler_params=_params(),
        cost_estimate=_cost(size),
    )(core, *sources)


def _split(v):
    high = v.astype(jnp.bfloat16)
    return high, (v - high.astype(jnp.float32)).astype(jnp.bfloat16)


def _dot3(a, b, dims):
    ah, al = _split(a)
    bh, bl = _split(b)

    def dot(p, q):
        return lax.dot_general(p, q, (dims, ((), ())), preferred_element_type=jnp.float32)

    return dot(ah, bh) + (dot(ah, bl) + dot(al, bh))


def _my_rows(r, k):
    return pl.ds(pl.multiple_of(r * 512 + k * 256, 256), 256)


def _half_rows(k):
    return pl.ds(pl.multiple_of(k * 256, 256), 256)


def _near(r, k, v, x0, q0, q1, x1):
    return [
        (0, lambda j: v.at[_my_rows(r, k), _rows(j)], None),
        (1, lambda j: x0.at[r, :, _rows(j)], None),
        (2, lambda j: q0.at[_half_rows(k), _rows(j % 4)], 0),
        (2, lambda j: q1.at[_half_rows(k), _rows(j % 4)], 1),
        (3, lambda j: x1.at[j // 4, :, _rows(j % 4)], None),
    ]


def beta_product(r, table, mine, other, v, x0, q0, q1, x1, early, late, extra):
    def kernel(table_ref, *refs):
        weights, ins, outs = refs[0:2], refs[2:-8], refs[-8:-6]
        buf, w_buf, out_buf, sem, w_sem, out_sem = refs[-6:]
        loads = [pltpu.make_async_copy(weights[i], w_buf.at[i], w_sem.at[i]) for i in range(2)]
        for copy in loads:
            copy.start()
        options = [
            _near(r, table_ref[0], *ins[0:5]),
            [(4 + i, lambda s, i=i: ins[5 + i].at[s, r], None) for i in range(3)],
            [(7 + i, lambda s, i=i: ins[8 + i].at[s], None) for i in range(3)],
        ]
        for n in range(len(EXTRA)):
            options.append([(10 + i, lambda s, i=i: ins[11 + i].at[s, r], None) for i in range(3 * n, 3 * n + 3)])

        def load(n, _):
            _fetch(table_ref[BETA_CODE + n], options, buf.at[n], sem.at[n])

        lax.fori_loop(0, 32, load, None)
        for copy in loads:
            copy.wait()
        stores = []
        for i in range(2):

            def block(h, _, i=i):
                n = 16 * i + 2 * h
                w = jnp.concatenate([w_buf[i, h, 0], w_buf[i, h, 1]], axis=1)
                _wait(buf.at[n], sem.at[n])
                _wait(buf.at[n + 1], sem.at[n + 1])
                blocks = jnp.concatenate([buf[n], buf[n + 1]], axis=1)
                out_buf[i, :, _rows(h)] = _dot3(blocks, w, ((1,), (1,)))

            for part in range(2):
                lax.fori_loop(4 * part, 4 * part + 4, block, None, unroll=2)
                columns = slice(512 * part, 512 * part + 512)
                copy = pltpu.make_async_copy(out_buf.at[i, :, columns], outs[i].at[:, columns], out_sem.at[2 * i + part])
                copy.start()
                stores.append(copy)
        for copy in stores:
            copy.wait()

    return pl.pallas_call(
        kernel,
        out_shape=[_f32(256, 1024)] * 2,
        in_specs=[SMEM] + [ANY] * (13 + len(extra)),
        out_specs=[ANY, ANY],
        scratch_shapes=[
            pltpu.VMEM((32, 256, B), jnp.float32),
            pltpu.VMEM((2, 8, 2, B, B), jnp.float32),
            pltpu.VMEM((2, 256, 1024), jnp.float32),
            pltpu.SemaphoreType.DMA((32,)),
            pltpu.SemaphoreType.DMA((2,)),
            pltpu.SemaphoreType.DMA((4,)),
        ],
        compiler_params=_params(),
        cost_estimate=_cost(8 * 2**20, 3 * 32 * 2 * 256 * B * B),
    )(table, mine, other, v, x0, q0, q1, x1, *early, *late, *extra)


def alpha_product(c, table, values, v, q0, q1, own, late, tail=None):
    width = 512 if tail is None else 1024
    extra = [] if tail is None else [tail[0], *tail[1], *tail[2]]

    def body(table_ref, weights, ins, more, out, buf, w_buf, out_buf, sem, w_sem, out_sem, sum_buf=None, part_buf=None):
        k = table_ref[0]
        w_load = pltpu.make_async_copy(weights, w_buf, w_sem.at[0])
        w_load.start()
        columns = pl.ds(c * 512, 512)
        options = [
            [
                (0, lambda j: ins[0].at[_rows(j), columns], None),
                (1, lambda j: ins[1].at[_rows(j % 4)], 0),
                (1, lambda j: ins[2].at[_rows(j % 4)], 1),
            ],
            [(2 + i, lambda s, i=i: ins[3 + i].at[s, :, columns], None) for i in range(3)],
            [(5 + i, lambda s, i=i: ins[6 + i].at[s], None) for i in range(3)],
        ]

        def load(n, _):
            _fetch(table_ref[ALPHA_CODE + n], options, buf.at[n], sem.at[n])

        lax.fori_loop(0, 16, load, None)
        loads = [w_load]
        if tail is not None:
            terms = [(more[0], part_buf)]
            for r in range(2):
                terms.append((more[1 + r], sum_buf.at[_my_rows(r, k)]))
                terms.append((more[3 + r], sum_buf.at[_my_rows(r, 1 - k)]))
            for n, (source, target) in enumerate(terms):
                copy = pltpu.make_async_copy(source, target, w_sem.at[1 + n])
                copy.start()
                loads.append(copy)
        for copy in loads:
            copy.wait()

        def block(g, _):
            w = jnp.concatenate([w_buf[g, 0], w_buf[g, 1]], axis=1)
            _wait(buf.at[2 * g], sem.at[2 * g])
            _wait(buf.at[2 * g + 1], sem.at[2 * g + 1])
            product = _dot3(w, jnp.concatenate([buf[2 * g], buf[2 * g + 1]], axis=0), ((1,), (0,)))
            here = _rows(g)
            if tail is None:
                out_buf[here] = product
            else:
                for n in range(2):
                    there = slice(n * 512, (n + 1) * 512)
                    alpha = product if n == c else part_buf[here]
                    out_buf[here, there] = alpha + sum_buf[here, there]
            pltpu.make_async_copy(out_buf.at[here], out.at[here], out_sem.at[g]).start()

        lax.fori_loop(0, 8, block, None, unroll=2)

        def finish(g, _):
            _wait(out_buf.at[_rows(g)], out_sem.at[g])

        lax.fori_loop(0, 8, finish, None)

    def kernel(table_ref, weights, *refs):
        more = len(extra)
        body(table_ref, weights, refs[0:9], refs[9 : 9 + more], *refs[9 + more :])

    scratch = [
        pltpu.VMEM((16, B, 512), jnp.float32),
        pltpu.VMEM((8, 2, B, B), jnp.float32),
        pltpu.VMEM((1024, width), jnp.float32),
        pltpu.SemaphoreType.DMA((16,)),
        pltpu.SemaphoreType.DMA((6,)),
        pltpu.SemaphoreType.DMA((8,)),
    ]
    if tail is not None:
        scratch += [pltpu.VMEM((1024, 1024), jnp.float32), pltpu.VMEM((1024, 512), jnp.float32)]
    return pl.pallas_call(
        kernel,
        out_shape=_f32(1024, width),
        in_specs=[SMEM] + [ANY] * (10 + len(extra)),
        out_specs=ANY,
        scratch_shapes=scratch,
        compiler_params=_params(),
        cost_estimate=_cost((7 if tail is None else 15) * 2**20, 3 * 16 * 2 * B * B * 512),
    )(table, values, v, q0, q1, *own, *late, *extra)


def sigma_here(v, alpha_values, beta_values, core, table, need):
    quadrants = [(0, 0), (1, 0), (0, 1), (1, 1)]

    def quadrant(ins, r, c):
        return ins[0].at[r * 512 : (r + 1) * 512, c * 512 : (c + 1) * 512]

    half, piece = _pick(
        core,
        [(2, 256, 1024), (512, 512)],
        [v],
        lambda ins, k: [(ins[0].at[_my_rows(r, 1 - k)], 0, r) for r in range(2)] + [(quadrant(ins, 0, 0), 1, None)],
    )
    x0 = _send(half, TO_CORE)
    pieces = _pick(
        core, [(512, 512)] * 3, [v], lambda ins, k: [(quadrant(ins, *q), n, None) for n, q in enumerate(quadrants[1:])]
    )
    zl = {(r, c): _send(p, TO_ZL) for (r, c), p in zip(quadrants, [piece, *pieces])}
    other_values = _send(beta_values, TO_CORE)

    out = _gather(table, ALPHA_OWN, (B, 1024), 3, [v], lambda ins, k: [[(0, lambda j: ins[0].at[_rows(j)], None)]])
    own = _send_all(out, TO_X)

    def early_options(ins, k):
        def of_v(j):
            return ins[0].at[:, _half_rows(k), _rows(j)]

        return [[(0, of_v, None), (1, lambda j: ins[1].at[:, :, _rows(j)], None)]]

    out = _gather(table, BETA_LISTS, (2, 256, B), EARLY, [v.reshape(2, 512, 1024), x0], early_options)
    early = _send_all(out, TO_Y)

    zh = {(r, c): _send(zl[(r, c)], TO_ZNEXT) for r, c in quadrants}

    x1, late, x_late = {}, {}, {}
    for r in range(2):
        (half,) = _pick(
            core,
            [(2, 256, 512)],
            [zl[(r, 0)], zl[(r, 1)]],
            lambda ins, k: [(ins[c].at[_half_rows(1 - k)], 0, c) for c in range(2)],
        )
        x1[r] = _send(half, TO_CORE)
    for n in range(2):
        out = _gather(
            table,
            ALPHA_LATE,
            (B, 512),
            3,
            [zh[(0, n)], zh[(1, n)]],
            lambda ins, k: [[(0, lambda j, i=i: ins[i].at[_rows(j % 4)], i) for i in range(2)]],
        )
        x_late[n] = _send_all(out, TO_X)
        out = _gather(
            table,
            BETA_LISTS + 3 * STARTS[1],
            (256, B),
            LATE,
            [v, x0, zl[(n, 0)], zl[(n, 1)], x1[n]],
            lambda ins, k, n=n: [_near(n, k, *ins)],
        )
        late[n] = _send_all(out, TO_Y)

    def send_extra(start, slots):
        halves = []
        for r in range(2):
            halves.append(
                _gather(
                    table,
                    BETA_LISTS + 3 * start,
                    (256, B),
                    slots,
                    [v, x0, zl[(r, 0)], zl[(r, 1)], x1[r]],
                    lambda ins, k, r=r: [_near(r, k, *ins)],
                )
            )
        return tuple(_send_all([jnp.stack(pair, axis=1) for pair in zip(*halves)], TO_Y))

    def skip_extra(slots):
        return tuple(jnp.zeros((slots, 2, 256, B), jnp.float32) for _ in HOPS)

    extra = []
    for start, slots in zip(STARTS[2:], EXTRA):
        extra += lax.cond(
            need > start,
            lambda start=start, slots=slots: send_extra(start, slots),
            lambda slots=slots: skip_extra(slots),
        )

    ours, theirs = [], []
    for r in range(2):
        a, b = beta_product(
            r, table, beta_values, other_values, v, x0, zl[(r, 0)], zl[(r, 1)], x1[r], early, late[r], extra
        )
        ours.append(a)
        theirs.append(_send(b, TO_CORE))
    part = alpha_product(0, table, alpha_values, v, zh[(0, 0)], zh[(1, 0)], own, x_late[0])
    return alpha_product(
        1, table, alpha_values, v, zh[(0, 1)], zh[(1, 1)], own, x_late[1], (part, ours, theirs)
    )


def per_device(vector, links_alpha, alpha_values, links_beta, beta_values):
    row, col = lax.axis_index("row"), lax.axis_index("col")
    x, zh = row // NZH, row % NZH
    zl, y, k = col // (NY * NK), (col // NK) % NY, col % NK
    *beta, need = beta_tables(links_beta, zl, y, k)
    core = k.reshape(1)
    table = jnp.concatenate([core, *alpha_tables(links_alpha, x, zh), *beta])
    return sigma_here(vector, alpha_values, beta_values, core, table, need)


def solution(mesh):
    placed = (P("row", "col"), P(), P("row", None, None, None), P(), P("col", None, None, None))
    return jax.shard_map(per_device, mesh=mesh, in_specs=placed, out_specs=P("row", "col"), check_vma=False)
```

```python
import jax
import jax.numpy as jnp
from jax import lax
from jax.experimental import pallas as pl
from jax.experimental.pallas import tpu as pltpu
from jax.sharding import PartitionSpec as P


B = 128
AXES = ("row", "col")
HOPS = (1, 2, 3)
STARTS, SLOTS = (0, 5, 11, 12), (5, 6, 1, 4)
EARLY, LATE, *EXTRA = SLOTS
ALPHA_ROW, BETA_ROW, CORE, NEED = 3, 7, 126, 127
NX, NZH, NZL, NY, NK = 4, 2, 2, 4, 2


def _index(x, zh, zl, y, k):
    return (x * NZH + zh) * (NZL * NY * NK) + (zl * NY + y) * NK + k


def _pairs(move):
    pairs = []
    for x in range(NX):
        for zh in range(NZH):
            for zl in range(NZL):
                for y in range(NY):
                    for k in range(NK):
                        here = (x, zh, zl, y, k)
                        pairs.append((_index(*here), _index(*move(*here))))
    return pairs


def _z_next(x, zh, zl, y, k):
    z = (2 * zh + zl + (1 if zl == 1 else -1)) % 4
    return (x, z // 2, z % 2, y, k)


TO_CORE = _pairs(lambda x, zh, zl, y, k: (x, zh, zl, y, 1 - k))
TO_ZL = _pairs(lambda x, zh, zl, y, k: (x, zh, 1 - zl, y, k))
TO_ZNEXT = _pairs(_z_next)
TO_X = {d: _pairs(lambda x, zh, zl, y, k, d=d: ((x + d) % NX, zh, zl, y, k)) for d in HOPS}
TO_Y = {d: _pairs(lambda x, zh, zl, y, k, d=d: (x, zh, zl, (y + d) % NY, k)) for d in HOPS}


def _send(value, pairs):
    return lax.ppermute(value, AXES, pairs)


def _send_all(payloads, routes):
    return [_send(value, routes[d]) for d, value in zip(HOPS, payloads)]


def _row_sum(v):
    return jnp.sum(v.astype(jnp.float32), axis=1, keepdims=True).astype(jnp.int32)


def _members(entries, count, lane):
    member = jnp.zeros((8, 128), jnp.int32)
    for n in range(count):
        member = jnp.where(entries[:, n : n + 1] == lane, 1, member)
    return member


def _ranks(member, group, lane):
    ahead, total, step = member, member, 1
    while step < group:
        ahead = ahead + jnp.where((lane & (group - 1)) >= step, pltpu.roll(ahead, step, 1), 0)
        total = total + jnp.where((lane & step) > 0, pltpu.roll(total, step, 1), pltpu.roll(total, 128 - step, 1))
        step *= 2
    return ahead - member, total


def _lookup(codes, entries):
    return jnp.take_along_axis(codes, entries, axis=1)


def _position():
    row, col = lax.axis_index("row"), lax.axis_index("col")
    return row >> 1, row & 1, col >> 3, (col >> 1) & 3, col & 1


def _tables(alpha_ref, beta_ref, out_ref, pad_ref):
    x, zh, zl, y, k = _position()
    lane = lax.broadcasted_iota(jnp.int32, (8, 128), 1)
    row = lax.broadcasted_iota(jnp.int32, (8, 128), 0)

    pad_ref[...] = jnp.zeros_like(pad_ref)
    pad_ref[0, :, 0:32] = beta_ref[...]
    pad_ref[1, :, 0:16] = alpha_ref[...]
    wanted = pad_ref[0]
    member = _members(wanted, 32, lane)
    rank, total = _ranks(member, 16, lane)
    source_y = (lane >> 4) & 3
    other = (lane >> 6) ^ (row >> 2)
    near = (other * 2 + (((lane >> 3) & 1) ^ k)) * 32 + (lane & 7)
    pos = jnp.where(other == 1, jnp.maximum(pltpu.roll(total, 64, 1), EARLY) + rank, rank)
    hop = ((row & 3) - source_y) & 3
    reach = jnp.where((hop > 0) & (member > 0), pos + 1, 0).astype(jnp.float32)
    need = jnp.max(jnp.max(reach, axis=1, keepdims=True), axis=0, keepdims=True).astype(jnp.int32)
    level, at = jnp.zeros_like(pos), pos
    for before, start in zip(STARTS, STARTS[1:]):
        level = level + jnp.where(pos >= start, 1, 0)
        at = at - jnp.where(pos >= start, start - before, 0)
    beta_codes = _lookup(jnp.where(hop == 0, near, (3 + hop + 3 * level) * 32 + at), wanted)
    sent = jnp.where((member > 0) & (source_y == y), pos, -1)
    beta_lists = jnp.zeros_like(pos)
    for n in range(16):
        beta_lists = jnp.where(lane == n, _row_sum(jnp.where(sent == n, near, 0)), beta_lists)

    wanted = pad_ref[1]
    member = _members(wanted, 16, lane)
    rank, _ = _ranks(member, 8, lane)
    other = ((lane >> 3) & 1) ^ (row & 1)
    hop = ((row >> 1) - (lane >> 4)) & 3
    alpha_codes = _lookup(jnp.where(hop == 0, other * 32 + (lane & 7), (1 + hop + 3 * other) * 32 + rank), wanted)
    sent = jnp.where((member > 0) & ((lane >> 4) == x), rank + 3 * other, -1)
    alpha_lists = jnp.zeros_like(pos)
    for n in range(6):
        alpha_lists = jnp.where(lane == n, _row_sum(jnp.where(sent == n, lane & 7, 0)), alpha_lists)

    def pick(v, at):
        return jnp.sum(jnp.where(row == at, v, 0).astype(jnp.float32), axis=0, keepdims=True).astype(jnp.int32)

    for n, hop in enumerate(HOPS):
        out_ref[n : n + 1] = pick(alpha_lists, ((x + hop) & 3) * 2 + zh)
        out_ref[4 + n : 5 + n] = pick(beta_lists, zl * 4 + ((y + hop) & 3))
    codes = pick(alpha_codes, x * 2 + zh)
    codes = jnp.where(lane[0:1] == NEED, need, codes)
    out_ref[ALPHA_ROW : ALPHA_ROW + 1] = jnp.where(lane[0:1] == CORE, k, codes)
    out_ref[BETA_ROW : BETA_ROW + 1] = pick(beta_codes, zl * 4 + y)


def route_table(links_alpha, links_beta):
    return pl.pallas_call(
        _tables,
        name="route_table",
        out_shape=jax.ShapeDtypeStruct((8, 128), jnp.int32),
        in_specs=[VMEM, VMEM],
        out_specs=VMEM,
        scratch_shapes=[pltpu.VMEM((2, 8, 128), jnp.int32)],
        compiler_params=_params(),
        cost_estimate=_cost(12288),
    )(links_alpha.reshape(8, 16), links_beta.reshape(8, 32))


def _rows(i):
    return pl.ds(pl.multiple_of(i * B, B), B)


def _fetch(code, options, dst, sem):
    place, at = code >> 5, code & 31
    for group in options:
        first, last = group[0][0], group[-1][0]

        @pl.when(jnp.logical_and(place >= first, place <= last))
        def _(group=group):
            for number, source, half in group:
                test = place == number
                if half is not None:
                    test = jnp.logical_and(test, (at >> 2) == half)

                @pl.when(test)
                def _(source=source):
                    pltpu.make_async_copy(source(at), dst, sem).start()


def _wait(ref, sem):
    pltpu.make_async_copy(ref, ref, sem).wait()


ANY = pl.BlockSpec(memory_space=pl.ANY)
SMEM = pl.BlockSpec(memory_space=pltpu.SMEM)
VMEM = pl.BlockSpec(memory_space=pltpu.VMEM)


def _f32(*shape):
    return jax.ShapeDtypeStruct(shape, jnp.float32)


def _params():
    return pltpu.CompilerParams(vmem_limit_bytes=63 * 2**20)


def _cost(bytes_, flops=0):
    return pl.CostEstimate(flops=flops, bytes_accessed=bytes_, transcendentals=0)


def _gather(table, first_row, start, slot_shape, slots, sources, options_of):
    count = 3 * slots

    def kernel(table_ref, *refs):
        ins, outs = refs[: len(sources)], refs[len(sources) : len(sources) + 3]
        buf, in_sem, out_sem = refs[len(sources) + 3 :]
        options = options_of(ins, table_ref[ALPHA_ROW, CORE])

        for hop in range(3):

            def load(s, _, hop=hop):
                n = hop * slots + s
                _fetch(table_ref[first_row + hop, start + s], options, buf.at[n], in_sem.at[n])

            lax.fori_loop(0, slots, load, None)
        for hop, out in enumerate(outs):

            def store(s, _, hop=hop, out=out):
                n = hop * slots + s
                _wait(buf.at[n], in_sem.at[n])
                pltpu.make_async_copy(buf.at[n], out.at[s], out_sem.at[n]).start()

            lax.fori_loop(0, slots, store, None)

        def finish(s, _):
            _wait(buf.at[s], out_sem.at[s])

        lax.fori_loop(0, count, finish, None)

    size = 4 * count
    for n in slot_shape:
        size *= n
    return pl.pallas_call(
        kernel,
        out_shape=[_f32(slots, *slot_shape)] * 3,
        in_specs=[SMEM] + [ANY] * len(sources),
        out_specs=[ANY] * 3,
        scratch_shapes=[
            pltpu.VMEM((count, *slot_shape), jnp.float32),
            pltpu.SemaphoreType.DMA((count,)),
            pltpu.SemaphoreType.DMA((count,)),
        ],
        compiler_params=_params(),
        cost_estimate=_cost(2 * size),
    )(table, *sources)


def _pick(shapes, sources, picks_of):
    def kernel(*refs):
        ins, outs = refs[: len(sources)], refs[len(sources) : len(sources) + len(shapes)]
        bufs = refs[len(sources) + len(shapes) : -2]
        in_sem, out_sem = refs[-2:]
        loads, stores = [], []
        for n, (source, number, at) in enumerate(picks_of(ins, _position()[4])):
            buf, out = bufs[number], outs[number]
            if at is not None:
                buf, out = buf.at[at], out.at[at]
            loads.append(pltpu.make_async_copy(source, buf, in_sem.at[n]))
            stores.append(pltpu.make_async_copy(buf, out, out_sem.at[n]))
        for copy in loads:
            copy.start()
        for load, store in zip(loads, stores):
            load.wait()
            store.start()
        for copy in stores:
            copy.wait()

    size = 0
    for shape in shapes:
        words = 1
        for n in shape:
            words *= n
        size += 8 * words
    return pl.pallas_call(
        kernel,
        out_shape=[_f32(*shape) for shape in shapes],
        in_specs=[ANY] * len(sources),
        out_specs=[ANY] * len(shapes),
        scratch_shapes=[pltpu.VMEM(shape, jnp.float32) for shape in shapes]
        + [pltpu.SemaphoreType.DMA((6,)), pltpu.SemaphoreType.DMA((6,))],
        compiler_params=_params(),
        cost_estimate=_cost(size),
    )(*sources)


def _split(v):
    high = v.astype(jnp.bfloat16)
    return high, (v - high.astype(jnp.float32)).astype(jnp.bfloat16)


def _dot3(a, b, dims):
    (da,), (db,) = dims
    ah, al = _split(a)
    bh, bl = _split(b)
    left, right = jnp.concatenate([al, ah, ah], axis=da), jnp.concatenate([bh, bl, bh], axis=db)
    return lax.dot_general(left, right, (dims, ((), ())), preferred_element_type=jnp.float32)


def _my_rows(r, k):
    return pl.ds(pl.multiple_of(r * 512 + k * 256, 256), 256)


def _half_rows(k):
    return pl.ds(pl.multiple_of(k * 256, 256), 256)


def _near(r, k, v, x0, q0, q1, x1):
    return [
        (0, lambda j: v.at[_my_rows(r, k), _rows(j)], None),
        (1, lambda j: x0.at[r, :, _rows(j)], None),
        (2, lambda j: q0.at[_half_rows(k), _rows(j & 3)], 0),
        (2, lambda j: q1.at[_half_rows(k), _rows(j & 3)], 1),
        (3, lambda j: x1.at[j >> 2, :, _rows(j & 3)], None),
    ]


def beta_product(r, table, mine, other, v, x0, q0, q1, x1, early, late, extra):
    def kernel(table_ref, *refs):
        weights, ins, outs = refs[0:2], refs[2:-8], refs[-8:-6]
        buf, w_buf, out_buf, sem, w_sem, out_sem = refs[-6:]
        k = table_ref[ALPHA_ROW, CORE]
        loads = [pltpu.make_async_copy(weights[i], w_buf.at[i], w_sem.at[i]) for i in range(2)]
        for copy in loads:
            copy.start()
        options = [
            _near(r, k, *ins[0:5]),
            [(4 + i, lambda s, i=i: ins[5 + i].at[s, r], None) for i in range(3)],
            [(7 + i, lambda s, i=i: ins[8 + i].at[s], None) for i in range(3)],
        ]
        for n in range(len(EXTRA)):
            options.append([(10 + i, lambda s, i=i: ins[11 + i].at[s, r], None) for i in range(3 * n, 3 * n + 3)])

        def load(n, _=None):
            _fetch(table_ref[BETA_ROW, (n + 16 * k) & 31], options, buf.at[n], sem.at[n])

        lax.fori_loop(0, 16, load, None)
        for copy in loads:
            copy.wait()
        stores = []
        for part in range(4):
            i = part >> 1
            for n in range(8 * part, 8 * part + 8):
                _wait(buf.at[n], sem.at[n])
            for h in range(4 * part, 4 * part + 4):
                n = 2 * h
                if n < 16:
                    load(n + 16)
                    load(n + 17)
                w = jnp.concatenate([w_buf[i, h & 7, 0], w_buf[i, h & 7, 1]], axis=1)
                blocks = jnp.concatenate([buf[n], buf[n + 1]], axis=1)
                out_buf[i, :, (h & 7) * B : (h & 7) * B + B] = _dot3(blocks, w, ((1,), (1,)))
            columns = slice(512 * (part & 1), 512 * (part & 1) + 512)
            copy = pltpu.make_async_copy(out_buf.at[i, :, columns], outs[i].at[:, columns], out_sem.at[part])
            copy.start()
            stores.append(copy)
        for copy in stores:
            copy.wait()

    return pl.pallas_call(
        kernel,
        out_shape=[_f32(256, 1024)] * 2,
        in_specs=[SMEM] + [ANY] * (13 + len(extra)),
        out_specs=[ANY, ANY],
        scratch_shapes=[
            pltpu.VMEM((32, 256, B), jnp.float32),
            pltpu.VMEM((2, 8, 2, B, B), jnp.float32),
            pltpu.VMEM((2, 256, 1024), jnp.float32),
            pltpu.SemaphoreType.DMA((32,)),
            pltpu.SemaphoreType.DMA((2,)),
            pltpu.SemaphoreType.DMA((4,)),
        ],
        compiler_params=_params(),
        cost_estimate=_cost(8 * 2**20, 3 * 32 * 2 * 256 * B * B),
    )(table, mine, other, v, x0, q0, q1, x1, *early, *late, *extra)


def fold(r, part, ours, theirs, total=None):
    def kernel(part_ref, ours_ref, theirs_ref, *refs):
        out = refs[-5]
        a_buf, s_buf, in_sem, out_sem = refs[-4:]
        k = _position()[4]
        shares = ((ours_ref, k), (theirs_ref, 1 - k))
        loads = []
        for n, (source, share) in enumerate(shares):
            loads.append(pltpu.make_async_copy(part_ref.at[_my_rows(r, share)], a_buf.at[n], in_sem.at[2 * n]))
            loads.append(pltpu.make_async_copy(source, s_buf.at[n], in_sem.at[2 * n + 1]))
        for copy in loads:
            copy.start()
        stores = []
        for n, (_, share) in enumerate(shares):
            loads[2 * n].wait()
            loads[2 * n + 1].wait()
            s_buf[n, :, 0:512] = s_buf[n, :, 0:512] + a_buf[n]
            stores.append(pltpu.make_async_copy(s_buf.at[n], out.at[_my_rows(r, share)], out_sem.at[n]))
            stores[n].start()
        for copy in stores:
            copy.wait()

    more = [] if total is None else [total]
    return pl.pallas_call(
        kernel,
        out_shape=_f32(1024, 1024),
        in_specs=[ANY] * (3 + len(more)),
        out_specs=ANY,
        scratch_shapes=[
            pltpu.VMEM((2, 256, 512), jnp.float32),
            pltpu.VMEM((2, 256, 1024), jnp.float32),
            pltpu.SemaphoreType.DMA((4,)),
            pltpu.SemaphoreType.DMA((2,)),
        ],
        input_output_aliases={3: 0} if more else {},
        compiler_params=_params(),
        cost_estimate=_cost(5 * 2**20),
    )(part, ours, theirs, *more)


def alpha_product(c, table, values, v, q0, q1, own, late, total=None):
    more = [] if total is None else [total]
    columns = pl.ds(c * 512, 512)

    def kernel(table_ref, weights, *refs):
        ins, out = refs[0:9], refs[9 + len(more)]
        buf, w_buf, out_buf, sem, w_sem, out_sem = refs[10 + len(more) :]
        loads = [pltpu.make_async_copy(weights, w_buf, w_sem.at[0])]
        if more:
            loads.append(pltpu.make_async_copy(refs[9].at[:, columns], out_buf, w_sem.at[1]))
        for copy in loads:
            copy.start()
        options = [
            [
                (0, lambda j: ins[0].at[_rows(j), columns], None),
                (1, lambda j: ins[1].at[_rows(j & 3)], 0),
                (1, lambda j: ins[2].at[_rows(j & 3)], 1),
            ],
            [(2 + i, lambda s, i=i: ins[3 + i].at[s, :, columns], None) for i in range(3)],
            [(5 + i, lambda s, i=i: ins[6 + i].at[s], None) for i in range(3)],
        ]

        def load(n, _=None):
            _fetch(table_ref[ALPHA_ROW, n], options, buf.at[n], sem.at[n])

        lax.fori_loop(0, 8, load, None)
        for copy in loads:
            copy.wait()
        stores = []
        for part in range(4):
            for n in range(4 * part, 4 * part + 4):
                _wait(buf.at[n], sem.at[n])
            for g in range(2 * part, 2 * part + 2):
                n = 2 * g
                if n < 8:
                    load(n + 8)
                    load(n + 9)
                w = jnp.concatenate([w_buf[g, 0], w_buf[g, 1]], axis=1)
                product = _dot3(w, jnp.concatenate([buf[n], buf[n + 1]], axis=0), ((1,), (0,)))
                here = slice(g * B, g * B + B)
                out_buf[here] = out_buf[here] + product if more else product
            here = slice(part * 256, part * 256 + 256)
            target = out.at[here, columns] if more else out.at[here]
            stores.append(pltpu.make_async_copy(out_buf.at[here], target, out_sem.at[part]))
            stores[part].start()
        for copy in stores:
            copy.wait()

    return pl.pallas_call(
        kernel,
        out_shape=_f32(1024, 1024 if more else 512),
        in_specs=[SMEM] + [ANY] * (10 + len(more)),
        out_specs=ANY,
        scratch_shapes=[
            pltpu.VMEM((16, B, 512), jnp.float32),
            pltpu.VMEM((8, 2, B, B), jnp.float32),
            pltpu.VMEM((1024, 512), jnp.float32),
            pltpu.SemaphoreType.DMA((16,)),
            pltpu.SemaphoreType.DMA((2,)),
            pltpu.SemaphoreType.DMA((4,)),
        ],
        input_output_aliases={11: 0} if more else {},
        compiler_params=_params(),
        cost_estimate=_cost((9 if more else 7) * 2**20, 3 * 16 * 2 * B * B * 512),
    )(table, values, v, q0, q1, *own, *late, *more)


def sigma_here(v, alpha_values, beta_values, table):
    need = table[ALPHA_ROW, NEED]

    quadrants = [(0, 0), (1, 0), (0, 1), (1, 1)]

    def quadrant(ins, r, c):
        return ins[0].at[r * 512 : (r + 1) * 512, c * 512 : (c + 1) * 512]

    half, *pieces = _pick(
        [(2, 256, 1024)] + [(512, 512)] * 3,
        [v],
        lambda ins, k: [(ins[0].at[_my_rows(r, 1 - k)], 0, r) for r in range(2)]
        + [(quadrant(ins, *q), 1 + n, None) for n, q in enumerate(quadrants[1:])],
    )
    x0 = _send(half, TO_CORE)
    zl = {(r, c): _send(p, TO_ZL) for (r, c), p in zip(quadrants, [v[:512, :512], *pieces])}
    other_values = _send(beta_values, TO_CORE)

    out = _gather(table, 0, 0, (B, 1024), 3, [v], lambda ins, k: [[(0, lambda j: ins[0].at[_rows(j)], None)]])
    own = _send_all(out, TO_X)

    def early_options(ins, k):
        def of_v(j):
            return ins[0].at[:, _half_rows(k), _rows(j)]

        return [[(0, of_v, None), (1, lambda j: ins[1].at[:, :, _rows(j)], None)]]

    out = _gather(table, 4, 0, (2, 256, B), EARLY, [v.reshape(2, 512, 1024), x0], early_options)
    early = _send_all(out, TO_Y)

    zh = {(r, c): _send(zl[(r, c)], TO_ZNEXT) for r, c in quadrants}

    x1, late, x_late = {}, {}, {}
    for r in range(2):
        (half,) = _pick(
            [(2, 256, 512)],
            [zl[(r, 0)], zl[(r, 1)]],
            lambda ins, k: [(ins[c].at[_half_rows(1 - k)], 0, c) for c in range(2)],
        )
        x1[r] = _send(half, TO_CORE)
    for n in range(2):
        out = _gather(
            table,
            0,
            3,
            (B, 512),
            3,
            [zh[(0, n)], zh[(1, n)]],
            lambda ins, k: [[(0, lambda j, i=i: ins[i].at[_rows(j & 3)], i) for i in range(2)]],
        )
        x_late[n] = _send_all(out, TO_X)
        out = _gather(
            table,
            4,
            STARTS[1],
            (256, B),
            LATE,
            [v, x0, zl[(n, 0)], zl[(n, 1)], x1[n]],
            lambda ins, k, n=n: [_near(n, k, *ins)],
        )
        late[n] = _send_all(out, TO_Y)

    def send_extra(start, slots):
        halves = []
        for r in range(2):
            halves.append(
                _gather(
                    table,
                    4,
                    start,
                    (256, B),
                    slots,
                    [v, x0, zl[(r, 0)], zl[(r, 1)], x1[r]],
                    lambda ins, k, r=r: [_near(r, k, *ins)],
                )
            )
        return tuple(_send_all([jnp.stack(pair, axis=1) for pair in zip(*halves)], TO_Y))

    def skip_extra(slots):
        shapes = tuple(_f32(slots, 2, 256, B) for _ in HOPS)
        return pl.pallas_call(lambda *refs: None, out_shape=shapes, out_specs=(ANY,) * 3)()

    extra = []
    for start, slots in zip(STARTS[2:], EXTRA):
        extra += lax.cond(
            need > start,
            lambda start=start, slots=slots: send_extra(start, slots),
            lambda slots=slots: skip_extra(slots),
        )

    part = alpha_product(0, table, alpha_values, v, zh[(0, 0)], zh[(1, 0)], own, x_late[0])
    total = None
    for r in range(2):
        ours, other = beta_product(
            r, table, beta_values, other_values, v, x0, zl[(r, 0)], zl[(r, 1)], x1[r], early, late[r], extra
        )
        total = fold(r, part, ours, _send(other, TO_CORE), total)
    return alpha_product(1, table, alpha_values, v, zh[(0, 1)], zh[(1, 1)], own, x_late[1], total)


def per_device(vector, links_alpha, alpha_values, links_beta, beta_values):
    table = route_table(links_alpha, links_beta)
    return sigma_here(vector, alpha_values, beta_values, table)


def solution(mesh):
    placed = (P("row", "col"), P(), P("row", None, None, None), P(), P("col", None, None, None))
    return jax.shard_map(per_device, mesh=mesh, in_specs=placed, out_specs=P("row", "col"), check_vma=False)
```

```python
import jax
import jax.numpy as jnp
from jax import lax
from jax.experimental import pallas as pl
from jax.experimental.pallas import tpu as pltpu
from jax.sharding import PartitionSpec as P


B = 128
AXES = ("row", "col")
HOPS = (1, 2, 3)
STARTS, SLOTS = (0, 5, 11, 12), (5, 6, 1, 4)
EARLY, LATE, *EXTRA = SLOTS
ALPHA_ROW, BETA_ROW, CORE, NEED = 3, 7, 126, 127
NX, NZH, NZL, NY, NK = 4, 2, 2, 4, 2


def _index(x, zh, zl, y, k):
    return (x * NZH + zh) * (NZL * NY * NK) + (zl * NY + y) * NK + k


def _pairs(move):
    pairs = []
    for x in range(NX):
        for zh in range(NZH):
            for zl in range(NZL):
                for y in range(NY):
                    for k in range(NK):
                        here = (x, zh, zl, y, k)
                        pairs.append((_index(*here), _index(*move(*here))))
    return pairs


def _z_next(x, zh, zl, y, k):
    z = (2 * zh + zl + (1 if zl == 1 else -1)) % 4
    return (x, z // 2, z % 2, y, k)


TO_CORE = _pairs(lambda x, zh, zl, y, k: (x, zh, zl, y, 1 - k))
TO_ZL = _pairs(lambda x, zh, zl, y, k: (x, zh, 1 - zl, y, k))
TO_ZNEXT = _pairs(_z_next)
TO_X = {d: _pairs(lambda x, zh, zl, y, k, d=d: ((x + d) % NX, zh, zl, y, k)) for d in HOPS}
TO_Y = {d: _pairs(lambda x, zh, zl, y, k, d=d: (x, zh, zl, (y + d) % NY, k)) for d in HOPS}


def _send(value, pairs):
    return lax.ppermute(value, AXES, pairs)


def _send_all(payloads, routes):
    return [_send(value, routes[d]) for d, value in zip(HOPS, payloads)]


def _row_sum(v):
    return jnp.sum(v.astype(jnp.float32), axis=1, keepdims=True).astype(jnp.int32)


def _members(entries, count, lane):
    member = jnp.zeros((8, 128), jnp.int32)
    for n in range(count):
        member = jnp.where(entries[:, n : n + 1] == lane, 1, member)
    return member


def _ranks(member, group, lane):
    ahead, total, step = member, member, 1
    while step < group:
        ahead = ahead + jnp.where((lane & (group - 1)) >= step, pltpu.roll(ahead, step, 1), 0)
        total = total + jnp.where((lane & step) > 0, pltpu.roll(total, step, 1), pltpu.roll(total, 128 - step, 1))
        step *= 2
    return ahead - member, total


def _lookup(codes, entries):
    return jnp.take_along_axis(codes, entries, axis=1)


def _position():
    row, col = lax.axis_index("row"), lax.axis_index("col")
    return row >> 1, row & 1, col >> 3, (col >> 1) & 3, col & 1


def _tables(alpha_ref, beta_ref, out_ref, pad_ref):
    x, zh, zl, y, k = _position()
    lane = lax.broadcasted_iota(jnp.int32, (8, 128), 1)
    row = lax.broadcasted_iota(jnp.int32, (8, 128), 0)

    pad_ref[...] = jnp.zeros_like(pad_ref)
    pad_ref[0, :, 0:32] = beta_ref[...]
    pad_ref[1, :, 0:16] = alpha_ref[...]
    wanted = pad_ref[0]
    member = _members(wanted, 32, lane)
    rank, total = _ranks(member, 16, lane)
    source_y = (lane >> 4) & 3
    other = (lane >> 6) ^ (row >> 2)
    near = (other * 2 + (((lane >> 3) & 1) ^ k)) * 32 + (lane & 7)
    pos = jnp.where(other == 1, jnp.maximum(pltpu.roll(total, 64, 1), EARLY) + rank, rank)
    hop = ((row & 3) - source_y) & 3
    reach = jnp.where((hop > 0) & (member > 0), pos + 1, 0).astype(jnp.float32)
    need = jnp.max(jnp.max(reach, axis=1, keepdims=True), axis=0, keepdims=True).astype(jnp.int32)
    level, at = jnp.zeros_like(pos), pos
    for before, start in zip(STARTS, STARTS[1:]):
        level = level + jnp.where(pos >= start, 1, 0)
        at = at - jnp.where(pos >= start, start - before, 0)
    beta_codes = _lookup(jnp.where(hop == 0, near, (3 + hop + 3 * level) * 32 + at), wanted)
    sent = jnp.where((member > 0) & (source_y == y), pos, -1)
    beta_lists = jnp.zeros_like(pos)
    for n in range(16):
        beta_lists = jnp.where(lane == n, _row_sum(jnp.where(sent == n, near, 0)), beta_lists)

    wanted = pad_ref[1]
    member = _members(wanted, 16, lane)
    rank, _ = _ranks(member, 8, lane)
    other = ((lane >> 3) & 1) ^ (row & 1)
    hop = ((row >> 1) - (lane >> 4)) & 3
    alpha_codes = _lookup(jnp.where(hop == 0, other * 32 + (lane & 7), (1 + hop + 3 * other) * 32 + rank), wanted)
    sent = jnp.where((member > 0) & ((lane >> 4) == x), rank + 3 * other, -1)
    alpha_lists = jnp.zeros_like(pos)
    for n in range(6):
        alpha_lists = jnp.where(lane == n, _row_sum(jnp.where(sent == n, lane & 7, 0)), alpha_lists)

    def pick(v, at):
        return jnp.sum(jnp.where(row == at, v, 0).astype(jnp.float32), axis=0, keepdims=True).astype(jnp.int32)

    for n, hop in enumerate(HOPS):
        out_ref[n : n + 1] = pick(alpha_lists, ((x + hop) & 3) * 2 + zh)
        out_ref[4 + n : 5 + n] = pick(beta_lists, zl * 4 + ((y + hop) & 3))
    codes = pick(alpha_codes, x * 2 + zh)
    codes = jnp.where(lane[0:1] == NEED, need, codes)
    out_ref[ALPHA_ROW : ALPHA_ROW + 1] = jnp.where(lane[0:1] == CORE, k, codes)
    out_ref[BETA_ROW : BETA_ROW + 1] = pick(beta_codes, zl * 4 + y)


def route_table(links_alpha, links_beta):
    return pl.pallas_call(
        _tables,
        name="route_table",
        out_shape=jax.ShapeDtypeStruct((8, 128), jnp.int32),
        in_specs=[VMEM, VMEM],
        out_specs=VMEM,
        scratch_shapes=[pltpu.VMEM((2, 8, 128), jnp.int32)],
        compiler_params=_params(),
        cost_estimate=_cost(12288),
    )(links_alpha.reshape(8, 16), links_beta.reshape(8, 32))


def _rows(i):
    return pl.ds(pl.multiple_of(i * B, B), B)


def _fetch(code, options, dst, sem):
    place, at = code >> 5, code & 31
    for group in options:
        first, last = group[0][0], group[-1][0]

        @pl.when(jnp.logical_and(place >= first, place <= last))
        def _(group=group):
            for number, source, half in group:
                test = place == number
                if half is not None:
                    test = jnp.logical_and(test, (at >> 2) == half)

                @pl.when(test)
                def _(source=source):
                    pltpu.make_async_copy(source(at), dst, sem).start()


def _wait(ref, sem):
    pltpu.make_async_copy(ref, ref, sem).wait()


ANY = pl.BlockSpec(memory_space=pl.ANY)
SMEM = pl.BlockSpec(memory_space=pltpu.SMEM)
VMEM = pl.BlockSpec(memory_space=pltpu.VMEM)


def _f32(*shape):
    return jax.ShapeDtypeStruct(shape, jnp.float32)


def _params(mib=16):
    return pltpu.CompilerParams(vmem_limit_bytes=mib * 2**20)


def _cost(bytes_, flops=0):
    return pl.CostEstimate(flops=flops, bytes_accessed=bytes_, transcendentals=0)


def _gather(table, first_row, start, slot_shape, slots, sources, options_of):
    count = 3 * slots

    def kernel(table_ref, *refs):
        ins, outs = refs[: len(sources)], refs[len(sources) : len(sources) + 3]
        buf, in_sem, out_sem = refs[len(sources) + 3 :]
        options = options_of(ins, table_ref[ALPHA_ROW, CORE])

        for hop in range(3):

            def load(s, _, hop=hop):
                n = hop * slots + s
                _fetch(table_ref[first_row + hop, start + s], options, buf.at[n], in_sem.at[n])

            lax.fori_loop(0, slots, load, None)
        for hop, out in enumerate(outs):

            def store(s, _, hop=hop, out=out):
                n = hop * slots + s
                _wait(buf.at[n], in_sem.at[n])
                pltpu.make_async_copy(buf.at[n], out.at[s], out_sem.at[n]).start()

            lax.fori_loop(0, slots, store, None)

        def finish(s, _):
            _wait(buf.at[s], out_sem.at[s])

        lax.fori_loop(0, count, finish, None)

    size = 4 * count
    for n in slot_shape:
        size *= n
    return pl.pallas_call(
        kernel,
        out_shape=[_f32(slots, *slot_shape)] * 3,
        in_specs=[SMEM] + [ANY] * len(sources),
        out_specs=[ANY] * 3,
        scratch_shapes=[
            pltpu.VMEM((count, *slot_shape), jnp.float32),
            pltpu.SemaphoreType.DMA((count,)),
            pltpu.SemaphoreType.DMA((count,)),
        ],
        compiler_params=_params(),
        cost_estimate=_cost(2 * size),
    )(table, *sources)


def _pick(shapes, sources, picks_of):
    def kernel(*refs):
        ins, outs = refs[: len(sources)], refs[len(sources) : len(sources) + len(shapes)]
        bufs = refs[len(sources) + len(shapes) : -2]
        in_sem, out_sem = refs[-2:]
        loads, stores = [], []
        for n, (source, number, at) in enumerate(picks_of(ins, _position()[4])):
            buf, out = bufs[number], outs[number]
            if at is not None:
                buf, out = buf.at[at], out.at[at]
            loads.append(pltpu.make_async_copy(source, buf, in_sem.at[n]))
            stores.append(pltpu.make_async_copy(buf, out, out_sem.at[n]))
        for copy in loads:
            copy.start()
        for load, store in zip(loads, stores):
            load.wait()
            store.start()
        for copy in stores:
            copy.wait()

    size = 0
    for shape in shapes:
        words = 1
        for n in shape:
            words *= n
        size += 8 * words
    return pl.pallas_call(
        kernel,
        out_shape=[_f32(*shape) for shape in shapes],
        in_specs=[ANY] * len(sources),
        out_specs=[ANY] * len(shapes),
        scratch_shapes=[pltpu.VMEM(shape, jnp.float32) for shape in shapes]
        + [pltpu.SemaphoreType.DMA((6,)), pltpu.SemaphoreType.DMA((6,))],
        compiler_params=_params(),
        cost_estimate=_cost(size),
    )(*sources)


def _split(v):
    high = v.astype(jnp.bfloat16)
    return high, (v - high.astype(jnp.float32)).astype(jnp.bfloat16)


def _dot3(a, b, dims):
    (da,), (db,) = dims
    ah, al = _split(a)
    bh, bl = _split(b)
    left, right = jnp.concatenate([al, ah, ah], axis=da), jnp.concatenate([bh, bl, bh], axis=db)
    return lax.dot_general(left, right, (dims, ((), ())), preferred_element_type=jnp.float32)


def _my_rows(r, k):
    return pl.ds(pl.multiple_of(r * 512 + k * 256, 256), 256)


def _half_rows(k):
    return pl.ds(pl.multiple_of(k * 256, 256), 256)


def _near(r, k, v, x0, q0, q1, x1):
    return [
        (0, lambda j: v.at[_my_rows(r, k), _rows(j)], None),
        (1, lambda j: x0.at[r, :, _rows(j)], None),
        (2, lambda j: q0.at[_half_rows(k), _rows(j & 3)], 0),
        (2, lambda j: q1.at[_half_rows(k), _rows(j & 3)], 1),
        (3, lambda j: x1.at[j >> 2, :, _rows(j & 3)], None),
    ]


def beta_product(r, table, mine, other, v, x0, q0, q1, x1, early, late, extra):
    def kernel(table_ref, *refs):
        weights, ins, outs = refs[0:2], refs[2:-8], refs[-8:-6]
        buf, w_buf, out_buf, sem, w_sem, out_sem = refs[-6:]
        k = table_ref[ALPHA_ROW, CORE]
        loads = [pltpu.make_async_copy(weights[i], w_buf.at[i], w_sem.at[i]) for i in range(2)]
        for copy in loads:
            copy.start()
        options = [
            _near(r, k, *ins[0:5]),
            [(4 + i, lambda s, i=i: ins[5 + i].at[s, r], None) for i in range(3)],
            [(7 + i, lambda s, i=i: ins[8 + i].at[s], None) for i in range(3)],
        ]
        for n in range(len(EXTRA)):
            options.append([(10 + i, lambda s, i=i: ins[11 + i].at[s, r], None) for i in range(3 * n, 3 * n + 3)])

        def load(n, _=None):
            _fetch(table_ref[BETA_ROW, (n + 16 * k) & 31], options, buf.at[n], sem.at[n])

        lax.fori_loop(0, 16, load, None)
        for copy in loads:
            copy.wait()
        stores = []
        for part in range(4):
            i = part >> 1
            for n in range(8 * part, 8 * part + 8):
                _wait(buf.at[n], sem.at[n])
            for h in range(4 * part, 4 * part + 4):
                n = 2 * h
                if n < 16:
                    load(n + 16)
                    load(n + 17)
                w = jnp.concatenate([w_buf[i, h & 7, 0], w_buf[i, h & 7, 1]], axis=1)
                blocks = jnp.concatenate([buf[n], buf[n + 1]], axis=1)
                out_buf[i, :, (h & 7) * B : (h & 7) * B + B] = _dot3(blocks, w, ((1,), (1,)))
            columns = slice(512 * (part & 1), 512 * (part & 1) + 512)
            copy = pltpu.make_async_copy(out_buf.at[i, :, columns], outs[i].at[:, columns], out_sem.at[part])
            copy.start()
            stores.append(copy)
        for copy in stores:
            copy.wait()

    return pl.pallas_call(
        kernel,
        out_shape=[_f32(256, 1024)] * 2,
        in_specs=[SMEM] + [ANY] * (13 + len(extra)),
        out_specs=[ANY, ANY],
        scratch_shapes=[
            pltpu.VMEM((32, 256, B), jnp.float32),
            pltpu.VMEM((2, 8, 2, B, B), jnp.float32),
            pltpu.VMEM((2, 256, 1024), jnp.float32),
            pltpu.SemaphoreType.DMA((32,)),
            pltpu.SemaphoreType.DMA((2,)),
            pltpu.SemaphoreType.DMA((4,)),
        ],
        compiler_params=_params(63),
        cost_estimate=_cost(8 * 2**20, 3 * 32 * 2 * 256 * B * B),
    )(table, mine, other, v, x0, q0, q1, x1, *early, *late, *extra)


def fold(r, part, ours, theirs, total=None):
    def kernel(part_ref, ours_ref, theirs_ref, *refs):
        out = refs[-5]
        a_buf, s_buf, in_sem, out_sem = refs[-4:]
        k = _position()[4]
        shares = ((ours_ref, k), (theirs_ref, 1 - k))
        loads = []
        for n, (source, share) in enumerate(shares):
            loads.append(pltpu.make_async_copy(part_ref.at[_my_rows(r, share)], a_buf.at[n], in_sem.at[2 * n]))
            loads.append(pltpu.make_async_copy(source, s_buf.at[n], in_sem.at[2 * n + 1]))
        for copy in loads:
            copy.start()
        stores = []
        for n, (_, share) in enumerate(shares):
            loads[2 * n].wait()
            loads[2 * n + 1].wait()
            s_buf[n, :, 0:512] = s_buf[n, :, 0:512] + a_buf[n]
            stores.append(pltpu.make_async_copy(s_buf.at[n], out.at[_my_rows(r, share)], out_sem.at[n]))
            stores[n].start()
        for copy in stores:
            copy.wait()

    more = [] if total is None else [total]
    return pl.pallas_call(
        kernel,
        out_shape=_f32(1024, 1024),
        in_specs=[ANY] * (3 + len(more)),
        out_specs=ANY,
        scratch_shapes=[
            pltpu.VMEM((2, 256, 512), jnp.float32),
            pltpu.VMEM((2, 256, 1024), jnp.float32),
            pltpu.SemaphoreType.DMA((4,)),
            pltpu.SemaphoreType.DMA((2,)),
        ],
        input_output_aliases={3: 0} if more else {},
        compiler_params=_params(63),
        cost_estimate=_cost(5 * 2**20),
    )(part, ours, theirs, *more)


def alpha_product(c, table, values, v, q0, q1, own, late, total=None):
    more = [] if total is None else [total]
    columns = pl.ds(c * 512, 512)

    def kernel(table_ref, weights, *refs):
        ins, out = refs[0:9], refs[9 + len(more)]
        buf, w_buf, out_buf, sem, w_sem, out_sem = refs[10 + len(more) :]
        loads = [pltpu.make_async_copy(weights, w_buf, w_sem.at[0])]
        if more:
            loads.append(pltpu.make_async_copy(refs[9].at[:, columns], out_buf, w_sem.at[1]))
        for copy in loads:
            copy.start()
        options = [
            [
                (0, lambda j: ins[0].at[_rows(j), columns], None),
                (1, lambda j: ins[1].at[_rows(j & 3)], 0),
                (1, lambda j: ins[2].at[_rows(j & 3)], 1),
            ],
            [(2 + i, lambda s, i=i: ins[3 + i].at[s, :, columns], None) for i in range(3)],
            [(5 + i, lambda s, i=i: ins[6 + i].at[s], None) for i in range(3)],
        ]

        def load(n, _=None):
            _fetch(table_ref[ALPHA_ROW, n], options, buf.at[n], sem.at[n])

        lax.fori_loop(0, 8, load, None)
        for copy in loads:
            copy.wait()
        stores = []
        for part in range(4):
            for n in range(4 * part, 4 * part + 4):
                _wait(buf.at[n], sem.at[n])
            for g in range(2 * part, 2 * part + 2):
                n = 2 * g
                if n < 8:
                    load(n + 8)
                    load(n + 9)
                w = jnp.concatenate([w_buf[g, 0], w_buf[g, 1]], axis=1)
                product = _dot3(w, jnp.concatenate([buf[n], buf[n + 1]], axis=0), ((1,), (0,)))
                here = slice(g * B, g * B + B)
                out_buf[here] = out_buf[here] + product if more else product
            here = slice(part * 256, part * 256 + 256)
            target = out.at[here, columns] if more else out.at[here]
            stores.append(pltpu.make_async_copy(out_buf.at[here], target, out_sem.at[part]))
            stores[part].start()
        for copy in stores:
            copy.wait()

    return pl.pallas_call(
        kernel,
        out_shape=_f32(1024, 1024 if more else 512),
        in_specs=[SMEM] + [ANY] * (10 + len(more)),
        out_specs=ANY,
        scratch_shapes=[
            pltpu.VMEM((16, B, 512), jnp.float32),
            pltpu.VMEM((8, 2, B, B), jnp.float32),
            pltpu.VMEM((1024, 512), jnp.float32),
            pltpu.SemaphoreType.DMA((16,)),
            pltpu.SemaphoreType.DMA((2,)),
            pltpu.SemaphoreType.DMA((4,)),
        ],
        input_output_aliases={11: 0} if more else {},
        compiler_params=_params(63),
        cost_estimate=_cost((9 if more else 7) * 2**20, 3 * 16 * 2 * B * B * 512),
    )(table, values, v, q0, q1, *own, *late, *more)


def sigma_here(v, alpha_values, beta_values, table):
    need = table[ALPHA_ROW, NEED]

    quadrants = [(0, 0), (1, 0), (0, 1), (1, 1)]

    def quadrant(ins, r, c):
        return ins[0].at[r * 512 : (r + 1) * 512, c * 512 : (c + 1) * 512]

    half, *pieces = _pick(
        [(2, 256, 1024)] + [(512, 512)] * 3,
        [v],
        lambda ins, k: [(ins[0].at[_my_rows(r, 1 - k)], 0, r) for r in range(2)]
        + [(quadrant(ins, *q), 1 + n, None) for n, q in enumerate(quadrants[1:])],
    )
    x0 = _send(half, TO_CORE)
    zl = {(r, c): _send(p, TO_ZL) for (r, c), p in zip(quadrants, [v[:512, :512], *pieces])}
    other_values = _send(beta_values, TO_CORE)

    out = _gather(table, 0, 0, (B, 1024), 3, [v], lambda ins, k: [[(0, lambda j: ins[0].at[_rows(j)], None)]])
    own = _send_all(out, TO_X)

    def early_options(ins, k):
        def of_v(j):
            return ins[0].at[:, _half_rows(k), _rows(j)]

        return [[(0, of_v, None), (1, lambda j: ins[1].at[:, :, _rows(j)], None)]]

    out = _gather(table, 4, 0, (2, 256, B), EARLY, [v.reshape(2, 512, 1024), x0], early_options)
    early = _send_all(out, TO_Y)

    zh = {(r, c): _send(zl[(r, c)], TO_ZNEXT) for r, c in quadrants}

    x1, late, x_late = {}, {}, {}
    for r in range(2):
        (half,) = _pick(
            [(2, 256, 512)],
            [zl[(r, 0)], zl[(r, 1)]],
            lambda ins, k: [(ins[c].at[_half_rows(1 - k)], 0, c) for c in range(2)],
        )
        x1[r] = _send(half, TO_CORE)
    for n in range(2):
        out = _gather(
            table,
            0,
            3,
            (B, 512),
            3,
            [zh[(0, n)], zh[(1, n)]],
            lambda ins, k: [[(0, lambda j, i=i: ins[i].at[_rows(j & 3)], i) for i in range(2)]],
        )
        x_late[n] = _send_all(out, TO_X)
        out = _gather(
            table,
            4,
            STARTS[1],
            (256, B),
            LATE,
            [v, x0, zl[(n, 0)], zl[(n, 1)], x1[n]],
            lambda ins, k, n=n: [_near(n, k, *ins)],
        )
        late[n] = _send_all(out, TO_Y)

    def send_extra(start, slots):
        halves = []
        for r in range(2):
            halves.append(
                _gather(
                    table,
                    4,
                    start,
                    (256, B),
                    slots,
                    [v, x0, zl[(r, 0)], zl[(r, 1)], x1[r]],
                    lambda ins, k, r=r: [_near(r, k, *ins)],
                )
            )
        return tuple(_send_all([jnp.stack(pair, axis=1) for pair in zip(*halves)], TO_Y))

    def skip_extra(slots):
        shapes = tuple(_f32(slots, 2, 256, B) for _ in HOPS)
        return pl.pallas_call(lambda *refs: None, out_shape=shapes, out_specs=(ANY,) * 3)()

    extra = []
    for start, slots in zip(STARTS[2:], EXTRA):
        extra += lax.cond(
            need > start,
            lambda start=start, slots=slots: send_extra(start, slots),
            lambda slots=slots: skip_extra(slots),
        )

    part = alpha_product(0, table, alpha_values, v, zh[(0, 0)], zh[(1, 0)], own, x_late[0])
    total = None
    for r in range(2):
        ours, other = beta_product(
            r, table, beta_values, other_values, v, x0, zl[(r, 0)], zl[(r, 1)], x1[r], early, late[r], extra
        )
        total = fold(r, part, ours, _send(other, TO_CORE), total)
    return alpha_product(1, table, alpha_values, v, zh[(0, 1)], zh[(1, 1)], own, x_late[1], total)


def per_device(vector, links_alpha, alpha_values, links_beta, beta_values):
    table = route_table(links_alpha, links_beta)
    return sigma_here(vector, alpha_values, beta_values, table)


def solution(mesh):
    placed = (P("row", "col"), P(), P("row", None, None, None), P(), P("col", None, None, None))
    return jax.shard_map(per_device, mesh=mesh, in_specs=placed, out_specs=P("row", "col"), check_vma=False)
```
